32 devices in a mesh: tm: 8 (over y, x, core), space: 4 (over z).
Axes of the slice: x: 2, y: 2, z: 4, core: 2. Of those that a mesh axis runs over, the one named last changes fastest.
Arguments:
- latents: float32 [8, 4, 32, 128], P('tm', None, 'space'), may hold values from -6 to 6
- owner_slot: int32 [1], replicated, may hold values from 0 to 7
- slot_steps: int32 [8], replicated, may hold values from 0 to 999
- step_table: float32 [1000], replicated, may hold values from 0.14 to 0.2
- mod_scale: float32 [1000, 320], replicated, may hold values from -3 to 3
- mod_shift: float32 [1000, 320], replicated, may hold values from -3 to 3
- w_in: bfloat16 [9, 320, 4], replicated, may hold values from -1 to 1
- w_one: bfloat16 [9, 320, 320], replicated, may hold values from -0.21875 to 0.21875
- w_two: bfloat16 [9, 320, 320], replicated, may hold values from -0.21875 to 0.21875
- w_out: bfloat16 [9, 4, 320], replicated, may hold values from -0.109375 to 0.109375
Outputs:
- iterates: float32 [8, 4, 32, 128], P('tm', None, 'space')
- window_end: float32 [4, 32, 128], P(None, 'space')
The draws below stay inside these ranges and needn't reach their ends.
Inputs may be any that keep to these rules, and one draw needn't show every extreme that they name: `owner_slot`: the slot that holds the window's start latent.
All inputs are finite; a program needn't handle non-finite values.
Results may differ from the reference program's by a relative error of at most 0.013.
Values may be sent and summed in bfloat16 or wider, within the bound.
No kernel may reach another device: no remote copies, remote signals or barrier semaphores. Data moves between devices by JAX's collectives and lax.ppermute only.
A program may use at most 64 MiB of HBM per device.

```python
import math
import jax
import jax.numpy as jnp
from jax import lax

CH = 320
LAT = 4
COLS = 128
TSTEPS = 1000
ITERS = 3
SLOTS = 8
ROWS = 32


def set_ends(drawn, own_key, low, top_value):
    index_at = [jax.random.randint(jax.random.fold_in(own_key, axis), (), 0, length) for axis, length in enumerate(drawn.shape)]
    main_axis = drawn.shape.index(max(drawn.shape))
    next_to = index_at[:main_axis] + [(index_at[main_axis] + 1) % drawn.shape[main_axis]] + index_at[main_axis + 1:]
    return drawn.at[tuple(index_at)].set(low).at[tuple(next_to)].set(top_value)


def steps_of(rng, extent, split, least, high):
    factor_of, own = 1.0, jax.random.fold_in(rng, 6)
    for axis_at, blocks in split:
        steps = jnp.exp(jax.random.uniform(jax.random.fold_in(own, axis_at), (blocks,), jnp.float32, least / len(split), high / len(split)))
        factor_of = factor_of * jnp.repeat(steps, extent[axis_at] // blocks).reshape([-1 if axis == axis_at else 1 for axis in range(len(extent))])
    return factor_of


def bell_draw(rng, dims, scale, bound, pieces=(), kind=jnp.bfloat16):
    loudness = steps_of(rng, dims, pieces, -0.22, 0.18) if pieces else 1.0
    values = jax.random.normal(rng, dims, jnp.float32) * scale * loudness
    return jnp.minimum(jnp.maximum(values, -bound), bound).astype(kind)


def setup_inputs(seed: int = 0) -> dict:
    splits = jax.random.split(jax.random.key(seed), 11)
    latents = bell_draw(splits[0], (SLOTS, LAT, ROWS, COLS), 1.0, 6.0, ((0, 8), (2, 4)), jnp.float32)
    owner_slot = jax.random.randint(splits[1], (1,), 0, SLOTS).astype(jnp.int32)
    slot_steps = set_ends(jax.random.randint(splits[2], (SLOTS,), 0, TSTEPS), jax.random.fold_in(splits[2], 1), 0, TSTEPS - 1).astype(jnp.int32)
    step_table = jnp.clip(jnp.exp(jax.random.uniform(splits[3], (TSTEPS,), jnp.float32, math.log(0.14), math.log(0.2))), 0.14, 0.2)
    mod_scale = bell_draw(splits[4], (TSTEPS, CH), 1.0, 3.0, (), jnp.float32)
    mod_shift = bell_draw(splits[5], (TSTEPS, CH), 0.5, 3.0, (), jnp.float32)
    w_in = bell_draw(splits[6], (9, CH, LAT), (9 * LAT) ** -0.5, 1.0)
    w_one = bell_draw(splits[7], (9, CH, CH), (9 * CH // 4) ** -0.5, 0.21875)
    w_two = bell_draw(splits[8], (9, CH, CH), (9 * CH // 4) ** -0.5, 0.21875)
    w_out = bell_draw(splits[9], (9, LAT, CH), (9 * CH) ** -0.5, 0.109375)
    return dict(latents=latents, owner_slot=owner_slot, slot_steps=slot_steps, step_table=step_table, mod_scale=mod_scale, mod_shift=mod_shift, w_in=w_in, w_one=w_one, w_two=w_two, w_out=w_out)


def conv_full(field_in, weight):
    row_count = field_in.shape[1]
    col_count = field_in.shape[2]
    padded = jnp.pad(field_in.astype(jnp.float32), ((0, 0), (1, 1), (1, 1)))
    summed = jnp.zeros((weight.shape[1], row_count, col_count), jnp.float32)
    for tap_index in range(9):
        row_off = tap_index // 3
        col_off = tap_index % 3
        summed = summed + jnp.einsum("oc,crw->orw", weight[tap_index].astype(jnp.float32),
                                     padded[:, row_off:row_off + row_count, col_off:col_off + col_count])
    return summed


def drift_block(iterate, scale_row, shift_row, w_in, w_one, w_two, w_out):
    state_in = iterate.astype(jnp.bfloat16)
    first_out = conv_full(state_in, w_in).astype(jnp.bfloat16)
    act_first = jax.nn.silu(first_out.astype(jnp.float32)).astype(jnp.bfloat16)
    inner_out = conv_full(act_first, w_one)
    modulated = jax.nn.silu(inner_out * (1.0 + scale_row[:, None, None]) + shift_row[:, None, None]).astype(jnp.bfloat16)
    second = (first_out.astype(jnp.float32) + conv_full(modulated, w_two)).astype(jnp.bfloat16)
    act_second = jax.nn.silu(second.astype(jnp.float32)).astype(jnp.bfloat16)
    return conv_full(act_second, w_out).astype(jnp.bfloat16)


def reference(latents, owner_slot, slot_steps, step_table, mod_scale, mod_shift, w_in, w_one, w_two, w_out):
    owner_index = owner_slot[0].astype(jnp.int32)
    slot_ids = jnp.arange(SLOTS, dtype=jnp.int32)
    window_pos = (slot_ids - owner_index) % SLOTS
    slot_order = (owner_index + slot_ids) % SLOTS
    x_start = lax.dynamic_index_in_dim(latents, owner_index, 0, keepdims=False)
    iterates = latents
    window_end = x_start
    step_sizes = step_table[slot_steps]
    for picard_step in range(ITERS):
        def one_slot(inputs):
            iterate, t_index = inputs
            return drift_block(iterate, mod_scale[t_index], mod_shift[t_index], w_in, w_one, w_two, w_out)

        drifts = lax.map(one_slot, (iterates, slot_steps))
        increments = step_sizes[:, None, None, None] * drifts.astype(jnp.float32)
        ordered = jnp.take(increments, slot_order, axis=0)
        inclusive = jnp.cumsum(ordered, axis=0)
        exclusive = jnp.concatenate([jnp.zeros_like(inclusive[:1]), inclusive[:-1]], axis=0)
        iterates = x_start[None] + jnp.take(exclusive, window_pos, axis=0)
        window_end = x_start + inclusive[-1]
    return iterates, window_end
```

```python
import functools

import jax
import jax.numpy as jnp
from jax import lax
from jax.experimental import pallas as pl
from jax.experimental.pallas import tpu as pltpu
from jax.sharding import PartitionSpec as P

ITERS = 3
HALO = 4
COLS = 128
F32, BF = jnp.float32, jnp.bfloat16
VMEM_SPEC = pl.BlockSpec(memory_space=pltpu.VMEM)
SMEM_SPEC = pl.BlockSpec(memory_space=pltpu.SMEM)
ANY_SPEC = pl.BlockSpec(memory_space=pl.ANY)


def silu(v):
    half = 0.5 * v
    return half + half * jnp.tanh(half)


def position(slot, owner, slots):
    return lax.rem(slot - owner + slots, slots)


def drift_kernel(first, slots, spaces, rows, owner_ref, steps_ref, table_ref, start_ref, sent_ref, scale_hbm, shift_hbm,
                 wi_ref, w1_hbm, w2_hbm, wo_ref, out_ref, w1, w2, mod, rem1, rem2, state, cols_in, keep, act_a, act_b,
                 acc, taps_out, wo, sems):
    chan = w1.shape[1]
    whole = chan // 256 * 256
    lat = out_ref.shape[0]
    slot, space = lax.axis_index("tm"), lax.axis_index("space")
    owner = owner_ref[0]
    t_step = steps_ref[slot]
    t_row = pl.multiple_of(t_step // 8 * 8, 8)
    copies = [
        pltpu.make_async_copy(scale_hbm.at[pl.ds(t_row, 8)], mod.at[0], sems.at[0]),
        pltpu.make_async_copy(shift_hbm.at[pl.ds(t_row, 8)], mod.at[1], sems.at[1]),
        pltpu.make_async_copy(w1_hbm, w1, sems.at[2]),
        pltpu.make_async_copy(w2_hbm, w2, sems.at[3]),
    ]
    for c in copies:
        c.start()
    lane = lax.broadcasted_iota(jnp.int32, (chan, COLS), 1)

    def inside(row):
        at = space * rows + row
        return jnp.where((at >= 0) & (at < spaces * rows), 1.0, 0.0).astype(F32)

    pieces = (
        (jnp.maximum(space - 1, 0), (rows - HALO) * COLS, HALO * COLS, 0, inside(-1)),
        (space, 0, rows * COLS, HALO * COLS, jnp.float32(1.0)),
        (jnp.minimum(space + 1, spaces - 1), 0, HALO * COLS, (rows + HALO) * COLS, inside(rows)),
    )
    for source, begin, width, put_at, weight in pieces:
        window = slice(begin, begin + width)
        if first:
            value = start_ref[slot, source, :, window].astype(F32)
        else:
            value = start_ref[owner, source, :, window].astype(F32)
            mine = position(slot, owner, slots)
            for q in range(slots):
                factor = jnp.where(position(q, owner, slots) < mine, table_ref[steps_ref[q]], 0.0)
                value = value + factor * sent_ref[q, source, :, window].astype(F32)
        state[:, put_at:put_at + width] = value.astype(BF).astype(F32) * weight

    def put(dst, row, v):
        dst[1, row] = v.astype(BF)
        dst[0, row] = jnp.where(lane == 0, 0.0, pltpu.roll(v, 1, 1)).astype(BF)
        dst[2, row] = jnp.where(lane == COLS - 1, 0.0, pltpu.roll(v, COLS - 1, 1)).astype(BF)

    n_in = rows + 6
    cols_in[...] = jnp.zeros_like(cols_in)
    lane4 = lax.broadcasted_iota(jnp.int32, (lat, COLS), 1)
    for r in range(rows + 2 * HALO):
        x = state[:, r * COLS:(r + 1) * COLS]
        shifted = (
            jnp.where(lane4 == 0, 0.0, pltpu.roll(x, 1, 1)),
            x,
            jnp.where(lane4 == COLS - 1, 0.0, pltpu.roll(x, COLS - 1, 1)),
        )
        for dr in range(3):
            if 0 <= r - dr < n_in:
                for dc in range(3):
                    k = (3 * dr + dc) * lat
                    cols_in[k:k + lat, (r - dr) * COLS:(r - dr + 1) * COLS] = shifted[dc]

    def first_layer(j, _):
        x = cols_in[:, pl.ds(pl.multiple_of(j * 256, 256), 256)].astype(BF)
        z = jnp.dot(wi_ref[...], x, preferred_element_type=F32).astype(BF)
        for h in range(2):
            zh = z[:, h * COLS:(h + 1) * COLS]
            row = 2 * j + h
            keep[row] = zh
            put(act_a, row, silu(zh.astype(F32)) * inside(row - 3))
        return 0

    lax.fori_loop(0, n_in // 2, first_layer, 0)

    def remainder(w):
        return jnp.concatenate([w[t, :, whole:] for t in range(9)], axis=1)

    def conv(src, w, rem, j):
        parts, total = [], None
        for t in range(9):
            dr, dc = t // 3, t % 3
            x = jnp.concatenate([src[dc, 2 * j + dr], src[dc, 2 * j + dr + 1]], axis=1)
            parts.append(x[whole:])
            p = jnp.dot(w[t, :, :whole], x[:whole], preferred_element_type=F32)
            total = p if total is None else total + p
        return total + jnp.dot(rem[...], jnp.concatenate(parts, axis=0), preferred_element_type=F32)

    def pipelined(src, w, rem, count, finish):
        acc[...] = conv(src, w, rem, 0)

        def step(j, _):
            new = conv(src, w, rem, j)
            finish(j - 1)
            acc[...] = new
            return 0

        lax.fori_loop(1, count, step, 0)
        finish(count - 1)

    def column(m):
        chosen = lax.broadcasted_iota(jnp.int32, (8, chan), 0) == lax.rem(t_step, 8)
        row = jnp.sum(jnp.where(chosen, m, 0.0), axis=0, keepdims=True)
        return jnp.transpose(jnp.broadcast_to(row, (8, chan)))[:, :1]

    copies[0].wait()
    copies[1].wait()
    scale, shift = 1.0 + column(mod[0]), column(mod[1])

    def finish_one(j):
        for h in range(2):
            row = 2 * j + h
            v = silu(acc[:, h * COLS:(h + 1) * COLS] * scale + shift)
            put(act_b, row, v * inside(row - 2))

    def finish_two(j):
        both = []
        for h in range(2):
            row = 2 * j + h
            second = (keep[row + 2].astype(F32) + acc[:, h * COLS:(h + 1) * COLS]).astype(BF).astype(F32)
            both.append((silu(second) * inside(row - 1)).astype(BF))
        taps_out[j] = jnp.dot(wo[...], jnp.concatenate(both, axis=1), preferred_element_type=F32)

    copies[2].wait()
    rem1[...] = remainder(w1)
    pipelined(act_a, w1, rem1, (rows + 4) // 2, finish_one)
    copies[3].wait()
    rem2[...] = remainder(w2)
    wo[...] = wo_ref[...]
    pipelined(act_b, w2, rem2, (rows + 2) // 2, finish_two)

    lane8 = lax.broadcasted_iota(jnp.int32, (8, COLS), 1)
    for r in range(rows):
        total = None
        for dr in range(3):
            q = r + dr
            p = taps_out[q // 2, :, (q % 2) * COLS:(q % 2 + 1) * COLS]
            for dc in range(3):
                t = 3 * dr + dc
                v = p[8 * t:8 * t + 8]
                if dc == 0:
                    v = jnp.where(lane8 == 0, 0.0, pltpu.roll(v, 1, 1))
                elif dc == 2:
                    v = jnp.where(lane8 == COLS - 1, 0.0, pltpu.roll(v, COLS - 1, 1))
                total = v if total is None else total + v
        out_ref[:, r * COLS:(r + 1) * COLS] = total[:lat].astype(BF)


def drift_call(first, slots, spaces, owner, steps, table, start, sent, scale, shift, wi, w1, w2, wo):
    chan, taps_k = wi.shape
    lat = start.shape[2]
    rows = start.shape[3] // COLS
    rest = 9 * (chan % 256)
    V = pltpu.VMEM
    return pl.pallas_call(
        functools.partial(drift_kernel, first, slots, spaces, rows),
        out_shape=jax.ShapeDtypeStruct((lat, rows * COLS), BF),
        in_specs=[SMEM_SPEC] * 3 + [VMEM_SPEC] * 2 + [ANY_SPEC] * 2 + [VMEM_SPEC, ANY_SPEC, ANY_SPEC, VMEM_SPEC],
        out_specs=VMEM_SPEC,
        scratch_shapes=[
            V(w1.shape, BF), V(w2.shape, BF), V((2, 8, chan), F32), V((chan, rest), BF), V((chan, rest), BF),
            V((lat, (rows + 8) * COLS), F32), V((taps_k, (rows + 6) * COLS), F32), V((rows + 6, chan, COLS), BF),
            V((3, rows + 6, chan, COLS), BF), V((3, rows + 4, chan, COLS), BF), V((chan, 256), F32),
            V(((rows + 2) // 2, wo.shape[0], 256), F32), V(wo.shape, BF), pltpu.SemaphoreType.DMA((4,)),
        ],
        compiler_params=pltpu.CompilerParams(vmem_limit_bytes=48 << 20),
        name="drift",
    )(owner, steps, table, start, sent, scale, shift, wi, w1, w2, wo)


def finish_kernel(slots, owner_ref, steps_ref, table_ref, got_ref, iterate_ref, end_ref):
    owner = owner_ref[0]
    mine = position(lax.axis_index("tm"), owner, slots)
    start = got_ref[owner, 1]
    lower, every = start, start
    for q in range(slots):
        size = table_ref[steps_ref[q]]
        drift = got_ref[q, 0]
        every = every + size * drift
        lower = lower + jnp.where(position(q, owner, slots) < mine, size, 0.0) * drift
    for r in range(iterate_ref.shape[2]):
        iterate_ref[0, :, r, :] = lower[:, r * COLS:(r + 1) * COLS]
        end_ref[:, r, :] = every[:, r * COLS:(r + 1) * COLS]


def to_everyone(value, axes, count):
    copies = jnp.broadcast_to(value[None], (count,) + value.shape)
    return lax.all_to_all(copies, axes, 0, 0)


def body(latents, owner_slot, slot_steps, step_table, mod_scale, mod_shift, w_in, w_one, w_two, w_out):
    slots, spaces = lax.axis_size("tm"), lax.axis_size("space")
    lat, rows = latents.shape[1], latents.shape[2]
    chan = w_one.shape[1]
    wi = jnp.pad(jnp.transpose(w_in, (1, 0, 2)).reshape(chan, 9 * lat), ((0, 0), (0, 48 - 9 * lat)))
    wo = jnp.pad(w_out, ((0, 0), (0, 8 - lat), (0, 0))).reshape(72, chan)
    flat = latents[0].reshape(lat, rows * COLS)

    def share(value):
        return to_everyone(value, ("tm", "space"), slots * spaces).reshape(slots, spaces, lat, rows * COLS)

    start = share(flat.astype(BF))
    sent = start
    for picard_step in range(ITERS):
        drift = drift_call(picard_step == 0, slots, spaces, owner_slot, slot_steps, step_table, start, sent,
                           mod_scale, mod_shift, wi, w_one, w_two, wo)
        if picard_step < ITERS - 1:
            sent = share(drift)
    got = to_everyone(jnp.stack([drift.astype(F32), flat]), "tm", slots)
    return pl.pallas_call(
        functools.partial(finish_kernel, slots),
        out_shape=(jax.ShapeDtypeStruct(latents.shape, F32), jax.ShapeDtypeStruct(latents.shape[1:], F32)),
        in_specs=[SMEM_SPEC] * 3 + [VMEM_SPEC],
        out_specs=(VMEM_SPEC, VMEM_SPEC),
        name="finish",
    )(owner_slot, slot_steps, step_table, got)


def solution(mesh):
    in_specs = (P("tm", None, "space", None), P(), P(), P(), P(), P(), P(), P(), P(), P())
    out_specs = (P("tm", None, "space", None), P(None, "space", None))
    return jax.shard_map(body, mesh=mesh, in_specs=in_specs, out_specs=out_specs, check_vma=False)
```

```python
import functools

import jax
import jax.numpy as jnp
from jax import lax
from jax.experimental import pallas as pl
from jax.experimental.pallas import tpu as pltpu
from jax.sharding import PartitionSpec as P

ITERS = 3
HALO = 4
COLS = 128
TAP_ROWS = 8
F32, BF = jnp.float32, jnp.bfloat16
VMEM_SPEC = pl.BlockSpec(memory_space=pltpu.VMEM)
SMEM_SPEC = pl.BlockSpec(memory_space=pltpu.SMEM)


def silu(v):
    half = 0.5 * v
    return half + half * jnp.tanh(half)


def position(slot, owner, slots):
    return lax.rem(slot - owner + slots, slots)


def factors_below(owner, steps_ref, table_ref, slot, slots):
    mine = position(slot, owner, slots)
    sizes = [jnp.where(position(q, owner, slots) < mine, table_ref[steps_ref[q]], 0.0) for q in range(slots)]
    return [jnp.where(owner == q, 1.0, sizes[q]) for q in range(slots)]


def weight_pieces(w, u):
    whole = w.shape[1] // 256 * 256
    rest = {}

    def piece(dc):
        top, mid, low = (w[3 * dr + dc].astype(F32) for dr in range(3))
        even, odd = 0.5 * (top + low), 0.5 * mid
        for i, v in enumerate((w[dc], (even + odd).astype(BF), (even - odd).astype(BF), w[6 + dc])):
            u[i, :, dc * whole:(dc + 1) * whole] = v[:, :whole]
            rest[i, dc] = v[:, whole:]
        if dc == 2:
            for i in range(4):
                u[i, :, 3 * whole:] = jnp.concatenate([rest[i, k] for k in range(3)], axis=1)

    return [functools.partial(piece, dc) for dc in range(3)]


def drift_kernel(first, last, copies, slots, spaces, rows, owner_ref, steps_ref, table_ref, own_ref, *refs):
    if first:
        (scale_hbm, shift_hbm, wi_in, wo_in, w1_hbm, w2_hbm, out_ref, *kept), refs = refs[:13], refs[13:]
        w1, w2, scale_all, shift_all, wi_rows, wo_rows, sems, *refs = refs
        loads = [pltpu.make_async_copy(src, dst, sems.at[n]) for n, (src, dst) in enumerate(
            ((w1_hbm, w1), (scale_hbm, scale_all), (shift_hbm, shift_all), (w2_hbm, w2)))]
        for load in loads:
            load.start()
    else:
        (sent_ref, *kept, out_ref), refs = refs[:8], refs[8:]
    scale_ref, shift_ref, wi_ref, wo_ref, u1, u2 = kept
    state, cols_in, keep, row_a, row_b, act_a, act_b, taps_out, prods = refs
    chan = scale_ref.shape[0]
    whole = chan // 256 * 256
    lat = out_ref.shape[-2]
    device_slot, space = lax.axis_index("tm"), lax.axis_index("space")
    owner = owner_ref[0]
    lane = lax.broadcasted_iota(jnp.int32, (chan, COLS), 1)

    def inside(row):
        at = space * rows + row
        return jnp.where((at >= 0) & (at < spaces * rows), 1.0, 0.0).astype(F32)

    before_one, beside_one = [], []
    if first:
        wi_rows[...] = jnp.zeros_like(wi_rows)
        wo_rows[...] = jnp.zeros_like(wo_rows)
        for t in range(9):
            wi_rows[t * lat:(t + 1) * lat, :chan] = wi_in[t].astype(F32)
            wo_rows[t * TAP_ROWS:t * TAP_ROWS + lat] = wo_in[t].astype(F32)
        wi_ref[...] = jnp.transpose(wi_rows[...])[:chan].astype(BF)
        wo_ref[...] = wo_rows[...].astype(BF)

        def modulation():
            t_step = steps_ref[device_slot]
            for load, src, dst, add in ((loads[1], scale_all, scale_ref, 1.0), (loads[2], shift_all, shift_ref, 0.0)):
                load.wait()
                chosen = lax.broadcasted_iota(jnp.int32, src.shape, 1) == t_step
                column = jnp.sum(jnp.where(chosen, src[...], 0.0), axis=1, keepdims=True)
                dst[...] = jnp.broadcast_to(column + add, dst.shape)

        before_one = [loads[0].wait] + weight_pieces(w1, u1)
        beside_one = [[modulation], [loads[3].wait] + weight_pieces(w2, u2)]

    if first:
        state[...] = own_ref[...].astype(BF).astype(F32)
    else:
        pieces = (
            (jnp.maximum(space - 1, 0), (rows - HALO) * COLS, HALO * COLS, 0, inside(-1)),
            (space, 0, rows * COLS, HALO * COLS, None),
            (jnp.minimum(space + 1, spaces - 1), 0, HALO * COLS, (rows + HALO) * COLS, inside(rows)),
        )
        factors = factors_below(owner, steps_ref, table_ref, device_slot, slots)
        for source, begin, width, put_at, weight in pieces:
            total = None
            for q in range(slots):
                term = factors[q] * sent_ref[q, source, :, begin:begin + width].astype(F32)
                total = term if total is None else total + term
            if weight is not None:
                total = total * weight
            value = jnp.where(device_slot == owner, own_ref[:, put_at:put_at + width], total)
            state[:, put_at:put_at + width] = value.astype(BF).astype(F32)

    n_in = rows + 6
    cols_in[...] = jnp.zeros_like(cols_in)
    lane4 = lax.broadcasted_iota(jnp.int32, (lat, COLS), 1)
    for r in range(rows + 2 * HALO):
        x = state[:, r * COLS:(r + 1) * COLS]
        shifted = (
            jnp.where(lane4 == 0, 0.0, pltpu.roll(x, 1, 1)),
            x,
            jnp.where(lane4 == COLS - 1, 0.0, pltpu.roll(x, COLS - 1, 1)),
        )
        for dr in range(3):
            if 0 <= r - dr < n_in:
                for dc in range(3):
                    k = (3 * dr + dc) * lat
                    cols_in[k:k + lat, (r - dr) * COLS:(r - dr + 1) * COLS] = shifted[dc]
    wi = wi_ref[:, :cols_in.shape[0]]

    def transformed(src, dst, p):
        r0, r1, r2, r3 = (src[2 * p + k] for k in range(4))
        for i, v in enumerate((r0 - r2, r1 + r2, r2 - r1, r1 - r3)):
            v = v.astype(BF)
            zero = jnp.zeros_like(v)
            dst[p, i, 1] = v
            dst[p, i, 0] = jnp.where(lane == 0, zero, pltpu.roll(v, 1, 1))
            dst[p, i, 2] = jnp.where(lane == COLS - 1, zero, pltpu.roll(v, COLS - 1, 1))

    def first_layer(j):
        x = cols_in[:, j * 256:(j + 1) * 256].astype(BF)
        z = jnp.dot(wi, x, preferred_element_type=F32).astype(BF)
        for h in range(2):
            zh = z[:, h * COLS:(h + 1) * COLS]
            row = 2 * j + h
            keep[row] = zh
            row_a[row] = silu(zh.astype(F32)) * inside(row - 3)
        if j:
            transformed(row_a, act_a, j - 1)

    def product(src, u, pairs, i):
        chunks = []
        for lo, hi in ((0, whole), (whole, chan)):
            for dc in range(3):
                chunks.append(jnp.concatenate([src[p, i, dc, lo:hi] for p in pairs], axis=1))
        return jnp.dot(u[i], jnp.concatenate(chunks, axis=0), preferred_element_type=F32)

    def conv(src, u, pairs, beside, slot):
        for i in range(4):
            prods[slot, i, :, :COLS * len(pairs)] = product(src, u, pairs, i)
            for work in beside[i * len(beside) // 4:(i + 1) * len(beside) // 4]:
                work()

    def untransformed(slot, row):
        at = slice(row // 2 * COLS, (row // 2 + 1) * COLS)
        if row % 2 == 0:
            return prods[slot, 0, :, at] + prods[slot, 1, :, at] + prods[slot, 2, :, at]
        return prods[slot, 1, :, at] - prods[slot, 2, :, at] - prods[slot, 3, :, at]

    def finish_one(row, slot, n):
        y = untransformed(slot, n)
        row_b[row] = silu(y * scale_ref[...] + shift_ref[...]) * inside(row - 2)
        if row >= 3 and row % 2:
            transformed(row_b, act_b, (row - 3) // 2)

    def finish_two(row, slot, n):
        y = untransformed(slot, n)
        second = (keep[row + 2].astype(F32) + y).astype(BF).astype(F32)
        act = (silu(second) * inside(row - 1)).astype(BF)
        taps_out[row] = jnp.dot(wo_ref[...], act, preferred_element_type=F32)

    pairs_one, pairs_two = (rows + 4) // 2, (rows + 2) // 2
    steps_one = [tuple(range(p, min(p + 2, pairs_one))) for p in range(0, pairs_one, 2)]
    steps_two = [tuple(range(p, min(p + 2, pairs_two))) for p in range(0, pairs_two, 2)]
    ready, slot = 0, 0
    waiting = []
    for pairs in steps_one:
        while ready <= pairs[-1] + 1:
            first_layer(ready)
            ready += 1
        for work in before_one:
            work()
        before_one = []
        beside = list(waiting)
        for j in range(ready, min(pairs[-1] + 4, pairs_one + 1)):
            beside.append(functools.partial(first_layer, j))
            ready = j + 1
        if beside_one:
            beside += beside_one.pop(0)
        conv(act_a, u1, pairs, beside, slot)
        waiting = [functools.partial(finish_one, 2 * pairs[0] + n, slot, n) for n in range(2 * len(pairs))]
        slot = 1 - slot
    done = 2 * steps_one[-1][0]
    for pairs in steps_two:
        if 2 * pairs[-1] + 3 >= done:
            for work in waiting:
                work()
            waiting, done = [], 2 * pairs_one
        conv(act_b, u2, pairs, waiting, slot)
        done = 2 * pairs_one
        waiting = [functools.partial(finish_two, 2 * pairs[0] + n, slot, n) for n in range(2 * len(pairs))]
        slot = 1 - slot
    for work in waiting:
        work()

    size = table_ref[steps_ref[device_slot]]
    lane8 = lax.broadcasted_iota(jnp.int32, (TAP_ROWS, COLS), 1)
    for r in range(rows):
        total = None
        for dc in range(3):
            v = None
            for dr in range(3):
                t = 3 * dr + dc
                p = taps_out[r + dr, TAP_ROWS * t:TAP_ROWS * (t + 1)]
                v = p if v is None else v + p
            if dc == 0:
                v = jnp.where(lane8 == 0, 0.0, pltpu.roll(v, 1, 1))
            elif dc == 2:
                v = jnp.where(lane8 == COLS - 1, 0.0, pltpu.roll(v, COLS - 1, 1))
            total = v if total is None else total + v
        drift = total[:lat].astype(BF).astype(F32)
        at = slice(r * COLS, (r + 1) * COLS)
        reached = own_ref[:, (r + HALO) * COLS:(r + HALO + 1) * COLS] + size * drift
        value = jnp.where(device_slot == owner, reached, drift)
        high = value.astype(BF)
        if last:
            low = (value - high.astype(F32)).astype(BF)
        for n in range(copies):
            if last:
                out_ref[n, 0, :, at] = high
                out_ref[n, 1, :, at] = low
            else:
                out_ref[n, :, at] = high


def drift_call(first, last, copies, slots, spaces, rows, chan, lat, tensors):
    V, S = pltpu.VMEM, jax.ShapeDtypeStruct
    hbm = pl.BlockSpec(memory_space=pltpu.HBM)
    padded = (chan + COLS - 1) // COLS * COLS
    outs = [S((copies, 2, lat, rows * COLS) if last else (copies, lat, rows * COLS), BF)]
    scratch = []
    specs = [SMEM_SPEC] * 3 + [VMEM_SPEC] * 8
    forms = [((chan, COLS), F32), ((chan, COLS), F32), ((chan, COLS), BF), ((9 * TAP_ROWS, chan), BF),
             ((4, chan, 3 * chan), BF), ((4, chan, 3 * chan), BF)]
    if first:
        specs = [SMEM_SPEC] * 3 + [VMEM_SPEC, hbm, hbm, VMEM_SPEC, VMEM_SPEC, hbm, hbm]
        outs += [V(*f) for f in forms]
        scratch = [V((9, chan, chan), BF), V((9, chan, chan), BF), V(tensors[4].shape, F32), V(tensors[5].shape, F32),
                   V((COLS, padded), F32), V((9 * TAP_ROWS, chan), F32), pltpu.SemaphoreType.DMA((4,))]
    scratch += [
        V((lat, (rows + 8) * COLS), F32), V((48, (rows + 6) * COLS), F32), V((rows + 6, chan, COLS), BF),
        V((rows + 6, chan, COLS), F32), V((rows + 4, chan, COLS), F32), V(((rows + 4) // 2, 4, 3, chan, COLS), BF),
        V(((rows + 2) // 2, 4, 3, chan, COLS), BF), V((rows + 2, 9 * TAP_ROWS, COLS), F32),
        V((2, 4, chan, 2 * COLS), F32),
    ]
    passes = 2 * chan * (3 * chan) * 2 * COLS * (rows + 4 + rows + 2)
    return pl.pallas_call(
        functools.partial(drift_kernel, first, last, copies, slots, spaces, rows),
        out_shape=outs,
        in_specs=specs,
        out_specs=[VMEM_SPEC] * len(outs),
        scratch_shapes=scratch,
        compiler_params=pltpu.CompilerParams(vmem_limit_bytes=(32 if first else 25) << 20),
        cost_estimate=pl.CostEstimate(flops=passes, transcendentals=36 * chan * COLS, bytes_accessed=6 << 20),
        name="drift",
    )(*tensors)


def finish_kernel(slots, owner_ref, steps_ref, table_ref, own_ref, sent_ref, iterate_ref, end_ref):
    owner = owner_ref[0]
    rows = iterate_ref.shape[2]
    slot = lax.axis_index("tm")
    below = factors_below(owner, steps_ref, table_ref, slot, slots)
    lower, every = None, None
    for q in range(slots):
        value = sent_ref[q, 0].astype(F32) + sent_ref[q, 1].astype(F32)
        low = below[q] * value
        full = jnp.where(owner == q, 1.0, table_ref[steps_ref[q]]) * value
        lower = low if lower is None else lower + low
        every = full if every is None else every + full
    lower = jnp.where(slot == owner, own_ref[:, HALO * COLS:(HALO + rows) * COLS], lower)
    for r in range(rows):
        iterate_ref[0, :, r, :] = lower[:, r * COLS:(r + 1) * COLS]
        end_ref[:, r, :] = every[:, r * COLS:(r + 1) * COLS]


def with_neighbour_rows(flat, width):
    count, index = lax.axis_size("space"), lax.axis_index("space")
    even = index % 2 == 0
    head, tail = flat[:, :width], flat[:, flat.shape[1] - width:]
    swap = lambda begin: [(i + a, i + 1 - a) for i in range(begin, count - 1, 2) for a in (0, 1)]
    one = lax.ppermute(jnp.where(even, tail, head), "space", swap(0))
    two = lax.ppermute(jnp.where(even, head, tail), "space", swap(1))
    return jnp.concatenate([jnp.where(even, two, one), flat, jnp.where(even, one, two)], axis=1)


def body(latents, owner_slot, slot_steps, step_table, mod_scale, mod_shift, w_in, w_one, w_two, w_out):
    slots, spaces = lax.axis_size("tm"), lax.axis_size("space")
    lat, rows = latents.shape[1], latents.shape[2]
    flat = latents[0].reshape(lat, rows * COLS)
    own = with_neighbour_rows(flat, HALO * COLS)
    call = functools.partial(drift_call, slots=slots, spaces=spaces, rows=rows, chan=w_one.shape[1], lat=lat)
    scalars = (owner_slot, slot_steps, step_table)
    everyone = slots * spaces
    stay = lambda a: pltpu.with_memory_space_constraint(a, pltpu.HBM)
    given = (stay(mod_scale.T), stay(mod_shift.T), jnp.transpose(w_in, (0, 2, 1)), w_out, stay(w_one), stay(w_two))
    drift, *weights = call(True, False, everyone, tensors=(*scalars, own, *given))
    for picard_step in range(1, ITERS):
        last = picard_step == ITERS - 1
        sent = lax.all_to_all(drift, ("tm", "space"), 0, 0).reshape(slots, spaces, lat, rows * COLS)
        drift, = call(False, last, slots if last else everyone, tensors=(*scalars, own, sent, *weights))
    sent = lax.all_to_all(drift, "tm", 0, 0)
    return pl.pallas_call(
        functools.partial(finish_kernel, slots),
        out_shape=(jax.ShapeDtypeStruct(latents.shape, F32), jax.ShapeDtypeStruct(latents.shape[1:], F32)),
        in_specs=[SMEM_SPEC] * 3 + [VMEM_SPEC] * 2,
        out_specs=(VMEM_SPEC, VMEM_SPEC),
        name="finish",
    )(*scalars, own, sent)


def solution(mesh):
    in_specs = (P("tm", None, "space", None), P(), P(), P(), P(), P(), P(), P(), P(), P())
    out_specs = (P("tm", None, "space", None), P(None, "space", None))
    return jax.shard_map(body, mesh=mesh, in_specs=in_specs, out_specs=out_specs, check_vma=False)
```

```python
import functools

import jax
import jax.numpy as jnp
from jax import lax
from jax.experimental import pallas as pl
from jax.experimental.pallas import tpu as pltpu
from jax.sharding import PartitionSpec as P

ITERS = 3
HALO = 4
COLS = 128
TAP_ROWS = 8
F32, BF = jnp.float32, jnp.bfloat16
VMEM_SPEC = pl.BlockSpec(memory_space=pltpu.VMEM)
SMEM_SPEC = pl.BlockSpec(memory_space=pltpu.SMEM)


def silu(half):
    return half + half * jnp.tanh(half)


def position(slot, owner, slots):
    return lax.rem(slot - owner + slots, slots)


def write_factors(out, owner_ref, steps_ref, table_ref, slot, slots):
    owner = owner_ref[0]
    mine = position(slot, owner, slots)
    owns = slot == owner
    values = []
    for q in range(slots):
        size = table_ref[steps_ref[q]]
        below = jnp.where(position(q, owner, slots) < mine, size, 0.0)
        values.append(jnp.where(owns, 0.0, jnp.where(owner == q, 1.0, below)))
    values += [jnp.where(owner == q, 1.0, table_ref[steps_ref[q]]) for q in range(slots)]
    one = jnp.where(owns, 1.0, 0.0)
    values += [one, jnp.where(owns, table_ref[steps_ref[slot]], 1.0), one]
    for n, value in enumerate(values):
        out[n] = jnp.full(out.shape[1:], value, F32)


def start_rows(space, if_even, if_odd):
    return [jnp.where(lax.rem(space, 2) == 0, if_even[:, k], if_odd[:, k]) for k in range(HALO)]


def weight_pieces(w, u):
    whole = w.shape[1] // 256 * 256
    rest = {}

    def piece(dc):
        top, mid, low = (w[3 * dr + dc].astype(F32) for dr in range(3))
        even, odd = 0.5 * (top + low), 0.5 * mid
        for i, v in enumerate((w[dc], (even + odd).astype(BF), (even - odd).astype(BF), w[6 + dc])):
            u[i, :, dc * whole:(dc + 1) * whole] = v[:, :whole]
            rest[i, dc] = v[:, whole:]
        if dc == 2:
            for i in range(4):
                u[i, :, 3 * whole:] = jnp.concatenate([rest[i, k] for k in range(3)], axis=1)

    return [functools.partial(piece, dc) for dc in range(3)]


def drift_kernel(first, last, copies, slots, spaces, rows, sent_one, sent_two, got_one, got_two, *refs):
    if first:
        (owner_ref, steps_ref, table_ref, scale_hbm, shift_hbm, wi_hbm, wo_hbm, w1_hbm, w2_hbm, out_ref, *kept) = refs[:17]
        (w1, w2, scale_all, shift_all, wi_in, wo_in, wi_rows, wo_rows, sems, *refs) = refs[17:]
        loads = [pltpu.make_async_copy(src, dst, sems.at[n]) for n, (src, dst) in enumerate(
            ((wi_hbm, wi_in), (wo_hbm, wo_in), (w1_hbm, w1), (scale_hbm, scale_all), (shift_hbm, shift_all), (w2_hbm, w2)))]
        for load in loads:
            load.start()
    else:
        (sent_ref, *kept, out_ref), refs = refs[:9], refs[9:]
    scale_ref, shift_ref, wi_ref, wo_ref, factors, u1, u2 = kept
    state, cols_in, keep, row_a, row_b, act_a, act_b, taps_out, prods = refs
    chan = scale_ref.shape[0]
    whole = chan // 256 * 256
    lat = out_ref.shape[-2]
    device_slot, space = lax.axis_index("tm"), lax.axis_index("space")
    lane = lax.broadcasted_iota(jnp.int32, (chan, COLS), 1)

    def masked(v, row):
        if 0 <= row < rows:
            return v
        at = space * rows + row
        return v * jnp.where((at >= 0) & (at < spaces * rows), 1.0, 0.0).astype(F32)

    before_one, beside_one = [], []
    if first:
        wi_rows[...] = jnp.zeros_like(wi_rows)
        wo_rows[...] = jnp.zeros_like(wo_rows)
        write_factors(factors, owner_ref, steps_ref, table_ref, device_slot, slots)
        loads[0].wait()
        loads[1].wait()
        for t in range(9):
            wi_rows[t * lat:(t + 1) * lat, :chan] = wi_in[t].astype(F32)
            wo_rows[t * TAP_ROWS:t * TAP_ROWS + lat] = wo_in[t].astype(F32)
        wi_ref[...] = jnp.transpose(wi_rows[...])[:chan].astype(BF)
        wo_ref[...] = wo_rows[...].astype(BF)

        def modulation():
            t_step = steps_ref[device_slot]
            loads[3].wait()
            loads[4].wait()
            for src, dst, add in ((scale_all, scale_ref, 1.0), (shift_all, shift_ref, 0.0)):
                chosen = lax.broadcasted_iota(jnp.int32, src.shape, 1) == t_step
                column = jnp.sum(jnp.where(chosen, src[...], 0.0), axis=1, keepdims=True)
                dst[...] = jnp.broadcast_to(0.5 * (column + add), dst.shape)

        before_one = [loads[2].wait] + weight_pieces(w1, u1)
        beside_one = [[modulation], [], [loads[5].wait] + weight_pieces(w2, u2)]

    own_rows = start_rows(space, got_two, got_one) + start_rows(space, sent_two, sent_one)
    own_rows += start_rows(space, sent_one, sent_two) + start_rows(space, got_one, got_two)
    for k, own in enumerate(own_rows):
        value = own
        if not first:
            row = k - HALO
            source = space
            if row < 0:
                source = jnp.maximum(space - 1, 0)
            elif row >= rows:
                source = jnp.minimum(space + 1, spaces - 1)
            at = slice(row % rows * COLS, (row % rows + 1) * COLS)
            total = None
            for q in range(slots):
                term = factors[q, :lat] * sent_ref[q, source, :, at].astype(F32)
                total = term if total is None else total + term
            value = masked(total, row) + factors[2 * slots, :lat] * own
        state[:, k * COLS:(k + 1) * COLS] = value.astype(BF).astype(F32)

    n_in = rows + 6
    cols_in[...] = jnp.zeros_like(cols_in)
    lane4 = lax.broadcasted_iota(jnp.int32, (lat, COLS), 1)
    for r in range(rows + 2 * HALO):
        x = state[:, r * COLS:(r + 1) * COLS]
        shifted = (
            jnp.where(lane4 == 0, 0.0, pltpu.roll(x, 1, 1)),
            x,
            jnp.where(lane4 == COLS - 1, 0.0, pltpu.roll(x, COLS - 1, 1)),
        )
        for dr in range(3):
            if 0 <= r - dr < n_in:
                for dc in range(3):
                    k = (3 * dr + dc) * lat
                    cols_in[k:k + lat, (r - dr) * COLS:(r - dr + 1) * COLS] = shifted[dc]
    wi = wi_ref[:, :cols_in.shape[0]]

    def transformed(src, dst, p):
        r0, r1, r2, r3 = (src[2 * p + k] for k in range(4))
        for i, v in enumerate((r0 - r2, r1 + r2, r2 - r1, r1 - r3)):
            v = v.astype(BF)
            zero = jnp.zeros_like(v)
            dst[p, i, 1] = v
            dst[p, i, 0] = jnp.where(lane == 0, zero, pltpu.roll(v, 1, 1))
            dst[p, i, 2] = jnp.where(lane == COLS - 1, zero, pltpu.roll(v, COLS - 1, 1))

    def first_layer(j):
        x = cols_in[:, j * 256:(j + 1) * 256].astype(BF)
        z = jnp.dot(wi, x, preferred_element_type=F32).astype(BF)
        for h in range(2):
            zh = z[:, h * COLS:(h + 1) * COLS]
            row = 2 * j + h
            keep[row] = zh
            row_a[row] = masked(silu(0.5 * zh.astype(F32)), row - 3)
        if j:
            transformed(row_a, act_a, j - 1)

    def product(src, u, pairs, i):
        chunks = []
        for lo, hi in ((0, whole), (whole, chan)):
            for dc in range(3):
                chunks.append(jnp.concatenate([src[p, i, dc, lo:hi] for p in pairs], axis=1))
        return jnp.dot(u[i], jnp.concatenate(chunks, axis=0), preferred_element_type=F32)

    def conv(src, u, pairs, beside, slot):
        for i in range(4):
            prods[slot, i, :, :COLS * len(pairs)] = product(src, u, pairs, i)
            for work in beside[i * len(beside) // 4:(i + 1) * len(beside) // 4]:
                work()

    def untransformed(slot, row):
        at = slice(row // 2 * COLS, (row // 2 + 1) * COLS)
        if row % 2 == 0:
            return prods[slot, 0, :, at] + prods[slot, 1, :, at] + prods[slot, 2, :, at]
        return prods[slot, 1, :, at] - prods[slot, 2, :, at] - prods[slot, 3, :, at]

    def finish_one(row, slot, n):
        y = untransformed(slot, n)
        row_b[row] = masked(silu(y * scale_ref[...] + shift_ref[...]), row - 2)
        if row >= 3 and row % 2:
            transformed(row_b, act_b, (row - 3) // 2)

    def finish_two(row, slot, n):
        y = untransformed(slot, n)
        second = (keep[row + 2].astype(F32) + y).astype(BF).astype(F32)
        act = masked(silu(0.5 * second), row - 1).astype(BF)
        taps_out[row] = jnp.dot(wo_ref[...], act, preferred_element_type=F32)

    pairs_one, pairs_two = (rows + 4) // 2, (rows + 2) // 2
    steps_one = [tuple(range(p, min(p + 2, pairs_one))) for p in range(0, pairs_one, 2)]
    steps_two = [tuple(range(p, min(p + 2, pairs_two))) for p in range(0, pairs_two, 2)]
    ready, slot = 0, 0
    waiting = []
    for pairs in steps_one:
        while ready <= pairs[-1] + 1:
            first_layer(ready)
            ready += 1
        for work in before_one:
            work()
        before_one = []
        beside = list(waiting)
        for j in range(ready, min(pairs[-1] + 4, pairs_one + 1)):
            beside.append(functools.partial(first_layer, j))
            ready = j + 1
        if beside_one:
            beside += beside_one.pop(0)
        conv(act_a, u1, pairs, beside, slot)
        waiting = [functools.partial(finish_one, 2 * pairs[0] + n, slot, n) for n in range(2 * len(pairs))]
        slot = 1 - slot
    done = 2 * steps_one[-1][0]
    for pairs in steps_two:
        if 2 * pairs[-1] + 3 >= done:
            for work in waiting:
                work()
            waiting, done = [], 2 * pairs_one
        conv(act_b, u2, pairs, waiting, slot)
        done = 2 * pairs_one
        waiting = [functools.partial(finish_two, 2 * pairs[0] + n, slot, n) for n in range(2 * len(pairs))]
        slot = 1 - slot
    for work in waiting:
        work()

    lane8 = lax.broadcasted_iota(jnp.int32, (TAP_ROWS, COLS), 1)
    for r in range(rows):
        total = None
        for dc in range(3):
            v = None
            for dr in range(3):
                t = 3 * dr + dc
                p = taps_out[r + dr, TAP_ROWS * t:TAP_ROWS * (t + 1)]
                v = p if v is None else v + p
            if dc == 0:
                v = jnp.where(lane8 == 0, 0.0, pltpu.roll(v, 1, 1))
            elif dc == 2:
                v = jnp.where(lane8 == COLS - 1, 0.0, pltpu.roll(v, COLS - 1, 1))
            total = v if total is None else total + v
        drift = total[:lat].astype(BF).astype(F32)
        at = slice(r * COLS, (r + 1) * COLS)
        value = factors[2 * slots + 1, :lat] * drift + factors[2 * slots + 2, :lat] * own_rows[HALO + r]
        high = value.astype(BF)
        if last:
            low = (value - high.astype(F32)).astype(BF)
        for n in range(copies):
            if last:
                out_ref[n, 0, :, at] = high
                out_ref[n, 1, :, at] = low
            else:
                out_ref[n, :, at] = high


def drift_call(first, last, copies, slots, spaces, rows, chan, lat, tensors):
    V, S = pltpu.VMEM, jax.ShapeDtypeStruct
    hbm = pl.BlockSpec(memory_space=pltpu.HBM)
    padded = (chan + COLS - 1) // COLS * COLS
    outs = [S((copies, 2, lat, rows * COLS) if last else (copies, lat, rows * COLS), BF)]
    scratch = []
    specs = [VMEM_SPEC] * 12
    if first:
        specs = [VMEM_SPEC] * 4 + [SMEM_SPEC] * 3 + [hbm] * 6
        outs += [V((chan, COLS), F32), V((chan, COLS), F32), V((chan, COLS), BF), V((9 * TAP_ROWS, chan), BF),
                 V((2 * slots + 3, 8, COLS), F32), V((4, chan, 3 * chan), BF), V((4, chan, 3 * chan), BF)]
        scratch = [V((9, chan, chan), BF), V((9, chan, chan), BF), V(tensors[7].shape, F32), V(tensors[8].shape, F32),
                   V(tensors[9].shape, BF), V(tensors[10].shape, BF), V((COLS, padded), F32),
                   V((9 * TAP_ROWS, chan), F32), pltpu.SemaphoreType.DMA((6,))]
    scratch += [
        V((lat, (rows + 8) * COLS), F32), V((48, (rows + 6) * COLS), F32), V((rows + 6, chan, COLS), BF),
        V((rows + 6, chan, COLS), F32), V((rows + 4, chan, COLS), F32), V(((rows + 4) // 2, 4, 3, chan, COLS), BF),
        V(((rows + 2) // 2, 4, 3, chan, COLS), BF), V((rows + 2, 9 * TAP_ROWS, COLS), F32),
        V((2, 4, chan, 2 * COLS), F32),
    ]
    passes = 2 * chan * (3 * chan) * 2 * COLS * (rows + 4 + rows + 2)
    return pl.pallas_call(
        functools.partial(drift_kernel, first, last, copies, slots, spaces, rows),
        out_shape=outs,
        in_specs=specs,
        out_specs=[VMEM_SPEC] * len(outs),
        scratch_shapes=scratch,
        compiler_params=pltpu.CompilerParams(vmem_limit_bytes=(32 if first else 25) << 20),
        cost_estimate=pl.CostEstimate(flops=passes, transcendentals=36 * chan * COLS, bytes_accessed=6 << 20),
        name="drift",
    )(*tensors)


def finish_kernel(slots, sent_one, sent_two, sent_ref, factors, iterate_ref, end_ref):
    rows, lat = iterate_ref.shape[2], iterate_ref.shape[1]
    space = lax.axis_index("space")
    own_rows = start_rows(space, sent_two, sent_one) + start_rows(space, sent_one, sent_two)
    for r in range(rows):
        at = slice(r * COLS, (r + 1) * COLS)
        lower, every = factors[2 * slots, :lat] * own_rows[r], None
        for q in range(slots):
            value = sent_ref[q, 0, :, at].astype(F32) + sent_ref[q, 1, :, at].astype(F32)
            full = factors[slots + q, :lat] * value
            lower = lower + factors[q, :lat] * value
            every = full if every is None else every + full
        iterate_ref[0, :, r, :] = lower
        end_ref[:, r, :] = every


def neighbour_rows(rows):
    count, index = lax.axis_size("space"), lax.axis_index("space")
    even = index % 2 == 0
    head, tail = rows[:, :HALO], rows[:, rows.shape[1] - HALO:]
    swap = lambda begin: [(i + a, i + 1 - a) for i in range(begin, count - 1, 2) for a in (0, 1)]
    one, two = jnp.where(even, tail, head), jnp.where(even, head, tail)
    return one, two, lax.ppermute(one, "space", swap(0)), lax.ppermute(two, "space", swap(1))


def body(latents, owner_slot, slot_steps, step_table, mod_scale, mod_shift, w_in, w_one, w_two, w_out):
    slots, spaces = lax.axis_size("tm"), lax.axis_size("space")
    lat, rows = latents.shape[1], latents.shape[2]
    assert rows == 2 * HALO
    state = neighbour_rows(latents[0])
    call = functools.partial(drift_call, slots=slots, spaces=spaces, rows=rows, chan=w_one.shape[1], lat=lat)
    everyone = slots * spaces
    stay = lambda a: pltpu.with_memory_space_constraint(a, pltpu.HBM)
    given = (mod_scale.T, mod_shift.T, jnp.transpose(w_in, (0, 2, 1)), w_out, w_one, w_two)
    drift, *weights = call(True, False, everyone, tensors=(
        *state, owner_slot, stay(slot_steps), stay(step_table), *(stay(a) for a in given)))
    for picard_step in range(1, ITERS):
        last = picard_step == ITERS - 1
        sent = lax.all_to_all(drift, ("tm", "space"), 0, 0).reshape(slots, spaces, lat, rows * COLS)
        drift, = call(False, last, slots if last else everyone, tensors=(*state, sent, *weights))
    sent = lax.all_to_all(drift, "tm", 0, 0)
    return pl.pallas_call(
        functools.partial(finish_kernel, slots),
        out_shape=(jax.ShapeDtypeStruct(latents.shape, F32), jax.ShapeDtypeStruct(latents.shape[1:], F32)),
        in_specs=[VMEM_SPEC] * 4,
        out_specs=(VMEM_SPEC, VMEM_SPEC),
        compiler_params=pltpu.CompilerParams(vmem_limit_bytes=4 << 20),
        name="finish",
    )(*state[:2], sent, weights[4])


def solution(mesh):
    in_specs = (P("tm", None, "space", None), P(), P(), P(), P(), P(), P(), P(), P(), P())
    out_specs = (P("tm", None, "space", None), P(None, "space", None))
    return jax.shard_map(body, mesh=mesh, in_specs=in_specs, out_specs=out_specs, check_vma=False)
```

```python
import functools

import jax
import jax.numpy as jnp
from jax import lax
from jax.experimental import pallas as pl
from jax.experimental.pallas import tpu as pltpu
from jax.sharding import PartitionSpec as P

ITERS = 3
HALO = 4
COLS = 128
TAP_ROWS = 8
F32, BF = jnp.float32, jnp.bfloat16
VMEM_SPEC = pl.BlockSpec(memory_space=pltpu.VMEM)
SMEM_SPEC = pl.BlockSpec(memory_space=pltpu.SMEM)


def silu(half):
    return half + half * jnp.tanh(half)


def position(slot, owner, slots):
    return lax.rem(slot - owner + slots, slots)


def write_factors(out, owner_ref, steps_ref, table_ref, slot, slots):
    owner = owner_ref[0]
    mine = position(slot, owner, slots)
    owns = slot == owner
    values = []
    for q in range(slots):
        size = table_ref[steps_ref[q]]
        below = jnp.where(position(q, owner, slots) < mine, size, 0.0)
        values.append(jnp.where(owns, 0.0, jnp.where(owner == q, 1.0, below)))
    values += [jnp.where(owner == q, 1.0, table_ref[steps_ref[q]]) for q in range(slots)]
    one = jnp.where(owns, 1.0, 0.0)
    values += [one, jnp.where(owns, table_ref[steps_ref[slot]], 1.0), one]
    for n, value in enumerate(values):
        out[n] = jnp.full(out.shape[1:], value, F32)


def start_rows(space, if_even, if_odd):
    return [jnp.where(lax.rem(space, 2) == 0, if_even[:, k], if_odd[:, k]) for k in range(HALO)]


def weight_pieces(w, u):
    whole = w.shape[1] // 256 * 256
    rest = {}

    def piece(dc):
        top, mid, low = (w[3 * dr + dc].astype(F32) for dr in range(3))
        even, odd = 0.5 * (top + low), 0.5 * mid
        for i, v in enumerate((w[dc], (even + odd).astype(BF), (even - odd).astype(BF), w[6 + dc])):
            u[i, :, dc * whole:(dc + 1) * whole] = v[:, :whole]
            rest[i, dc] = v[:, whole:]
        if dc == 2:
            for i in range(4):
                u[i, :, 3 * whole:] = jnp.concatenate([rest[i, k] for k in range(3)], axis=1)

    return [functools.partial(piece, dc) for dc in range(3)]


def prep_kernel(slots, owner_ref, steps_hbm, table_hbm, scale_hbm, shift_hbm, wi_hbm, wo_hbm, w1_hbm, w2_hbm,
                scale_ref, shift_ref, wi_ref, wo_ref, factors, u1, u2, steps_ref, table_ref, w1, w2, block, tail,
                wi_in, wo_in, wi_rows, wo_rows, sems):
    loads = [pltpu.make_async_copy(src, dst, sems.at[n]) for n, (src, dst) in enumerate(
        ((steps_hbm, steps_ref), (w1_hbm, w1), (wi_hbm, wi_in), (wo_hbm, wo_in), (w2_hbm, w2), (table_hbm, table_ref)))]
    for load in loads:
        load.start()
    blocks = scale_hbm.shape[1] // COLS
    loads[0].wait()
    t_step = steps_ref[lax.axis_index("tm")]
    begin = pl.multiple_of(jnp.minimum(t_step // COLS, blocks - 1) * COLS, COLS)
    columns = []
    for n, src in enumerate((scale_hbm, shift_hbm)):
        columns.append(pltpu.make_async_copy(src.at[:, pl.ds(begin, COLS)], block.at[n], sems.at[6 + 2 * n]))
        columns.append(pltpu.make_async_copy(src.at[:, blocks * COLS:], tail.at[n], sems.at[7 + 2 * n]))
    for load in columns:
        load.start()
    chan, lat = w1.shape[1], wi_in.shape[1]
    slot = lax.axis_index("tm")
    wi_rows[...] = jnp.zeros_like(wi_rows)
    wo_rows[...] = jnp.zeros_like(wo_rows)
    for load in loads[1:4]:
        load.wait()
    for t in range(9):
        wi_rows[t * lat:(t + 1) * lat, :chan] = wi_in[t].astype(F32)
        wo_rows[t * TAP_ROWS:t * TAP_ROWS + lat] = wo_in[t].astype(F32)
    wi_ref[...] = jnp.transpose(wi_rows[...])[:chan].astype(BF)
    wo_ref[...] = wo_rows[...].astype(BF)
    for work in weight_pieces(w1, u1):
        work()
    for load in loads[4:] + columns:
        load.wait()
    for work in weight_pieces(w2, u2):
        work()
    write_factors(factors, owner_ref, steps_ref, table_ref, slot, slots)
    for n, (dst, add) in enumerate(((scale_ref, 1.0), (shift_ref, 0.0))):
        column = None
        for ref, first in ((block, begin), (tail, blocks * COLS)):
            chosen = lax.broadcasted_iota(jnp.int32, ref.shape[1:], 1) + first == t_step
            part = jnp.sum(jnp.where(chosen, ref[n], 0.0), axis=1, keepdims=True)
            column = part if column is None else column + part
        dst[...] = jnp.broadcast_to(0.5 * (column + add), dst.shape)


def prep_call(slots, chan, scalars, given):
    V = pltpu.VMEM
    padded = (chan + COLS - 1) // COLS * COLS
    stay = lambda a: pltpu.with_memory_space_constraint(a, pltpu.HBM)
    scale, shift, wi, wo, w1, w2 = given
    return pl.pallas_call(
        functools.partial(prep_kernel, slots),
        out_shape=[V((chan, COLS), F32), V((chan, COLS), F32), V((chan, COLS), BF), V((9 * TAP_ROWS, chan), BF),
                   V((2 * slots + 3, 8, COLS), F32), V((4, chan, 3 * chan), BF), V((4, chan, 3 * chan), BF)],
        in_specs=[SMEM_SPEC] + [pl.BlockSpec(memory_space=pltpu.HBM)] * 8,
        out_specs=[VMEM_SPEC] * 7,
        scratch_shapes=[pltpu.SMEM(scalars[1].shape, jnp.int32), pltpu.SMEM(scalars[2].shape, F32), V(w1.shape, BF),
                        V(w2.shape, BF), V((2, chan, COLS), F32), V((2, chan, scale.shape[1] % COLS), F32), V(wi.shape, BF),
                        V(wo.shape, BF), V((COLS, padded), F32), V((9 * TAP_ROWS, chan), F32),
                        pltpu.SemaphoreType.DMA((10,))],
        compiler_params=pltpu.CompilerParams(vmem_limit_bytes=16 << 20),
        cost_estimate=pl.CostEstimate(flops=1 << 20, transcendentals=0, bytes_accessed=8 << 20),
        name="prep",
    )(scalars[0], *(stay(a) for a in scalars[1:]), *(stay(a) for a in given))


def drift_kernel(first, last, copies, slots, spaces, rows, sent_one, sent_two, got_one, got_two, *refs):
    if not first:
        sent_ref, *refs = refs
    (*kept, out_ref), refs = refs[:8], refs[8:]
    scale_ref, shift_ref, wi_ref, wo_ref, factors, u1, u2 = kept
    state, cols_in, keep, row_a, row_b, act_a, act_b, taps_out, prods = refs
    chan = scale_ref.shape[0]
    whole = chan // 256 * 256
    lat = out_ref.shape[-2]
    device_slot, space = lax.axis_index("tm"), lax.axis_index("space")
    lane = lax.broadcasted_iota(jnp.int32, (chan, COLS), 1)

    def masked(v, row):
        if 0 <= row < rows:
            return v
        at = space * rows + row
        return v * jnp.where((at >= 0) & (at < spaces * rows), 1.0, 0.0).astype(F32)

    own_rows = start_rows(space, got_two, got_one) + start_rows(space, sent_two, sent_one)
    own_rows += start_rows(space, sent_one, sent_two) + start_rows(space, got_one, got_two)
    for k, own in enumerate(own_rows):
        value = own
        if not first:
            row = k - HALO
            source = space
            if row < 0:
                source = jnp.maximum(space - 1, 0)
            elif row >= rows:
                source = jnp.minimum(space + 1, spaces - 1)
            at = slice(row % rows * COLS, (row % rows + 1) * COLS)
            total = None
            for q in range(slots):
                term = factors[q, :lat] * sent_ref[q, source, :, at].astype(F32)
                total = term if total is None else total + term
            value = masked(total, row) + factors[2 * slots, :lat] * own
        state[:, k * COLS:(k + 1) * COLS] = value.astype(BF).astype(F32)

    n_in = rows + 6
    cols_in[...] = jnp.zeros_like(cols_in)
    lane4 = lax.broadcasted_iota(jnp.int32, (lat, COLS), 1)
    for r in range(rows + 2 * HALO):
        x = state[:, r * COLS:(r + 1) * COLS]
        shifted = (
            jnp.where(lane4 == 0, 0.0, pltpu.roll(x, 1, 1)),
            x,
            jnp.where(lane4 == COLS - 1, 0.0, pltpu.roll(x, COLS - 1, 1)),
        )
        for dr in range(3):
            if 0 <= r - dr < n_in:
                for dc in range(3):
                    k = (3 * dr + dc) * lat
                    cols_in[k:k + lat, (r - dr) * COLS:(r - dr + 1) * COLS] = shifted[dc]
    wi = wi_ref[:, :cols_in.shape[0]]

    def transformed(src, dst, p):
        r0, r1, r2, r3 = (src[2 * p + k] for k in range(4))
        for i, v in enumerate((r0 - r2, r1 + r2, r2 - r1, r1 - r3)):
            v = v.astype(BF)
            zero = jnp.zeros_like(v)
            dst[p, i, 1] = v
            dst[p, i, 0] = jnp.where(lane == 0, zero, pltpu.roll(v, 1, 1))
            dst[p, i, 2] = jnp.where(lane == COLS - 1, zero, pltpu.roll(v, COLS - 1, 1))

    def first_layer(j):
        x = cols_in[:, j * 256:(j + 1) * 256].astype(BF)
        z = jnp.dot(wi, x, preferred_element_type=F32).astype(BF)
        for h in range(2):
            zh = z[:, h * COLS:(h + 1) * COLS]
            row = 2 * j + h
            keep[row] = zh
            row_a[row] = masked(silu(0.5 * zh.astype(F32)), row - 3)
        if j:
            transformed(row_a, act_a, j - 1)

    def product(src, u, pairs, i):
        chunks = []
        for lo, hi in ((0, whole), (whole, chan)):
            for dc in range(3):
                chunks.append(jnp.concatenate([src[p, i, dc, lo:hi] for p in pairs], axis=1))
        return jnp.dot(u[i], jnp.concatenate(chunks, axis=0), preferred_element_type=F32)

    def conv(src, u, pairs, beside, slot):
        for i in range(4):
            prods[slot, i, :, :COLS * len(pairs)] = product(src, u, pairs, i)
            for work in beside[i * len(beside) // 4:(i + 1) * len(beside) // 4]:
                work()

    def untransformed(slot, row):
        at = slice(row // 2 * COLS, (row // 2 + 1) * COLS)
        if row % 2 == 0:
            return prods[slot, 0, :, at] + prods[slot, 1, :, at] + prods[slot, 2, :, at]
        return prods[slot, 1, :, at] - prods[slot, 2, :, at] - prods[slot, 3, :, at]

    def finish_one(row, slot, n):
        y = untransformed(slot, n)
        row_b[row] = masked(silu(y * scale_ref[...] + shift_ref[...]), row - 2)
        if row >= 3 and row % 2:
            transformed(row_b, act_b, (row - 3) // 2)

    def finish_two(row, slot, n):
        y = untransformed(slot, n)
        second = (keep[row + 2].astype(F32) + y).astype(BF).astype(F32)
        act = masked(silu(0.5 * second), row - 1).astype(BF)
        taps_out[row] = jnp.dot(wo_ref[...], act, preferred_element_type=F32)

    pairs_one, pairs_two = (rows + 4) // 2, (rows + 2) // 2
    steps_one = [tuple(range(p, min(p + 2, pairs_one))) for p in range(0, pairs_one, 2)]
    steps_two = [tuple(range(p, min(p + 2, pairs_two))) for p in range(0, pairs_two, 2)]
    ready, slot = 0, 0
    waiting = []
    for pairs in steps_one:
        while ready <= pairs[-1] + 1:
            first_layer(ready)
            ready += 1
        beside = list(waiting)
        for j in range(ready, min(pairs[-1] + 4, pairs_one + 1)):
            beside.append(functools.partial(first_layer, j))
            ready = j + 1
        conv(act_a, u1, pairs, beside, slot)
        waiting = [functools.partial(finish_one, 2 * pairs[0] + n, slot, n) for n in range(2 * len(pairs))]
        slot = 1 - slot
    done = 2 * steps_one[-1][0]
    for pairs in steps_two:
        if 2 * pairs[-1] + 3 >= done:
            for work in waiting:
                work()
            waiting, done = [], 2 * pairs_one
        conv(act_b, u2, pairs, waiting, slot)
        done = 2 * pairs_one
        waiting = [functools.partial(finish_two, 2 * pairs[0] + n, slot, n) for n in range(2 * len(pairs))]
        slot = 1 - slot
    for work in waiting:
        work()

    lane8 = lax.broadcasted_iota(jnp.int32, (TAP_ROWS, COLS), 1)
    for r in range(rows):
        total = None
        for dc in range(3):
            v = None
            for dr in range(3):
                t = 3 * dr + dc
                p = taps_out[r + dr, TAP_ROWS * t:TAP_ROWS * (t + 1)]
                v = p if v is None else v + p
            if dc == 0:
                v = jnp.where(lane8 == 0, 0.0, pltpu.roll(v, 1, 1))
            elif dc == 2:
                v = jnp.where(lane8 == COLS - 1, 0.0, pltpu.roll(v, COLS - 1, 1))
            total = v if total is None else total + v
        drift = total[:lat].astype(BF).astype(F32)
        at = slice(r * COLS, (r + 1) * COLS)
        value = factors[2 * slots + 1, :lat] * drift + factors[2 * slots + 2, :lat] * own_rows[HALO + r]
        high = value.astype(BF)
        if last:
            low = (value - high.astype(F32)).astype(BF)
        for n in range(copies):
            if last:
                out_ref[n, 0, :, at] = high
                out_ref[n, 1, :, at] = low
            else:
                out_ref[n, :, at] = high


def drift_call(first, last, copies, slots, spaces, rows, chan, lat, tensors):
    V = pltpu.VMEM
    out = jax.ShapeDtypeStruct((copies, 2, lat, rows * COLS) if last else (copies, lat, rows * COLS), BF)
    scratch = [
        V((lat, (rows + 8) * COLS), F32), V((48, (rows + 6) * COLS), F32), V((rows + 6, chan, COLS), BF),
        V((rows + 6, chan, COLS), F32), V((rows + 4, chan, COLS), F32), V(((rows + 4) // 2, 4, 3, chan, COLS), BF),
        V(((rows + 2) // 2, 4, 3, chan, COLS), BF), V((rows + 2, 9 * TAP_ROWS, COLS), F32),
        V((2, 4, chan, 2 * COLS), F32),
    ]
    passes = 2 * chan * (3 * chan) * 2 * COLS * (rows + 4 + rows + 2)
    return pl.pallas_call(
        functools.partial(drift_kernel, first, last, copies, slots, spaces, rows),
        out_shape=out,
        in_specs=[VMEM_SPEC] * len(tensors),
        out_specs=VMEM_SPEC,
        scratch_shapes=scratch,
        compiler_params=pltpu.CompilerParams(vmem_limit_bytes=25 << 20),
        cost_estimate=pl.CostEstimate(flops=passes, transcendentals=36 * chan * COLS, bytes_accessed=6 << 20),
        name="drift",
    )(*tensors)


def finish_kernel(slots, sent_one, sent_two, sent_ref, factors, iterate_ref, end_ref):
    rows, lat = iterate_ref.shape[2], iterate_ref.shape[1]
    space = lax.axis_index("space")
    own_rows = start_rows(space, sent_two, sent_one) + start_rows(space, sent_one, sent_two)
    for r in range(rows):
        at = slice(r * COLS, (r + 1) * COLS)
        lower, every = factors[2 * slots, :lat] * own_rows[r], None
        for q in range(slots):
            value = sent_ref[q, 0, :, at].astype(F32) + sent_ref[q, 1, :, at].astype(F32)
            full = factors[slots + q, :lat] * value
            lower = lower + factors[q, :lat] * value
            every = full if every is None else every + full
        iterate_ref[0, :, r, :] = lower
        end_ref[:, r, :] = every


def neighbour_rows(rows):
    count, index = lax.axis_size("space"), lax.axis_index("space")
    even = index % 2 == 0
    head, tail = rows[:, :HALO], rows[:, rows.shape[1] - HALO:]
    swap = lambda begin: [(i + a, i + 1 - a) for i in range(begin, count - 1, 2) for a in (0, 1)]
    one, two = jnp.where(even, tail, head), jnp.where(even, head, tail)
    return one, two, lax.ppermute(one, "space", swap(0)), lax.ppermute(two, "space", swap(1))


def body(latents, owner_slot, slot_steps, step_table, mod_scale, mod_shift, w_in, w_one, w_two, w_out):
    slots, spaces = lax.axis_size("tm"), lax.axis_size("space")
    lat, rows = latents.shape[1], latents.shape[2]
    assert rows == 2 * HALO
    state = neighbour_rows(latents[0])
    call = functools.partial(drift_call, slots=slots, spaces=spaces, rows=rows, chan=w_one.shape[1], lat=lat)
    everyone = slots * spaces
    weights = prep_call(slots, w_one.shape[1], (owner_slot, slot_steps, step_table), (
        mod_scale.T, mod_shift.T, jnp.transpose(w_in, (0, 2, 1)), w_out, w_one, w_two))
    drift = call(True, False, everyone, tensors=(*state, *weights))
    for picard_step in range(1, ITERS):
        last = picard_step == ITERS - 1
        sent = lax.all_to_all(drift, ("tm", "space"), 0, 0).reshape(slots, spaces, lat, rows * COLS)
        drift = call(False, last, slots if last else everyone, tensors=(*state, sent, *weights))
    sent = lax.all_to_all(drift, "tm", 0, 0)
    return pl.pallas_call(
        functools.partial(finish_kernel, slots),
        out_shape=(jax.ShapeDtypeStruct(latents.shape, F32), jax.ShapeDtypeStruct(latents.shape[1:], F32)),
        in_specs=[VMEM_SPEC] * 4,
        out_specs=(VMEM_SPEC, VMEM_SPEC),
        compiler_params=pltpu.CompilerParams(vmem_limit_bytes=4 << 20),
        name="finish",
    )(*state[:2], sent, weights[4])


def solution(mesh):
    in_specs = (P("tm", None, "space", None), P(), P(), P(), P(), P(), P(), P(), P(), P())
    out_specs = (P("tm", None, "space", None), P(None, "space", None))
    return jax.shard_map(body, mesh=mesh, in_specs=in_specs, out_specs=out_specs, check_vma=False)
```

```python
import functools

import jax
import jax.numpy as jnp
from jax import lax
from jax.experimental import pallas as pl
from jax.experimental.pallas import tpu as pltpu
from jax.sharding import PartitionSpec as P

ITERS = 3
HALO = 4
COLS = 128
TAP_ROWS = 8
F32, BF = jnp.float32, jnp.bfloat16
VMEM_SPEC = pl.BlockSpec(memory_space=pltpu.VMEM)
SMEM_SPEC = pl.BlockSpec(memory_space=pltpu.SMEM)


def silu(half):
    return half + half * jnp.tanh(half)


def position(slot, owner, slots):
    return lax.rem(slot - owner + slots, slots)


def write_factors(out, owner_ref, steps_ref, table_ref, slot, slots):
    owner = owner_ref[0]
    mine = position(slot, owner, slots)
    owns = slot == owner
    values = []
    for q in range(slots):
        size = table_ref[steps_ref[q]]
        below = jnp.where(position(q, owner, slots) < mine, size, 0.0)
        values.append(jnp.where(owns, 0.0, jnp.where(owner == q, 1.0, below)))
    values += [jnp.where(owner == q, 1.0, table_ref[steps_ref[q]]) for q in range(slots)]
    one = jnp.where(owns, 1.0, 0.0)
    values += [one, jnp.where(owns, table_ref[steps_ref[slot]], 1.0), one]
    for n, value in enumerate(values):
        out[n] = jnp.full(out.shape[1:], value, F32)


def start_rows(space, if_even, if_odd):
    return [jnp.where(lax.rem(space, 2) == 0, if_even[:, k], if_odd[:, k]) for k in range(HALO)]


def weight_pieces(w, u):
    whole = w.shape[1] // 256 * 256
    rest = {}

    def piece(dc):
        top, mid, low = (w[3 * dr + dc].astype(F32) for dr in range(3))
        even, odd = 0.5 * (top + low), 0.5 * mid
        for i, v in enumerate((w[dc], (even + odd).astype(BF), (even - odd).astype(BF), w[6 + dc])):
            u[i, :, dc * whole:(dc + 1) * whole] = v[:, :whole]
            rest[i, dc] = v[:, whole:]
        if dc == 2:
            for i in range(4):
                u[i, :, 3 * whole:] = jnp.concatenate([rest[i, k] for k in range(3)], axis=1)

    return [functools.partial(piece, dc) for dc in range(3)]


def prep_kernel(slots, owner_ref, steps_hbm, table_hbm, scale_hbm, shift_hbm, wi_hbm, wo_hbm, w1_hbm, w2_hbm,
                scale_ref, shift_ref, wi_ref, wo_ref, factors, u1, u2, steps_ref, table_ref, w1, w2, block, tail,
                wi_in, wo_in, wi_rows, wo_rows, sems):
    loads = [pltpu.make_async_copy(src, dst, sems.at[n]) for n, (src, dst) in enumerate(
        ((steps_hbm, steps_ref), (wi_hbm, wi_in), (wo_hbm, wo_in), (table_hbm, table_ref)))]
    taps = {(n, dc): [pltpu.make_async_copy(src.at[3 * dr + dc], dst.at[3 * dr + dc], sems.at[10 + 9 * n + 3 * dc + dr])
                      for dr in range(3)] for n, (src, dst) in enumerate(((w1_hbm, w1), (w2_hbm, w2))) for dc in range(3)}
    for load in loads + sum(taps.values(), []):
        load.start()
    blocks = scale_hbm.shape[1] // COLS
    loads[0].wait()
    t_step = steps_ref[lax.axis_index("tm")]
    begin = pl.multiple_of(jnp.minimum(t_step // COLS, blocks - 1) * COLS, COLS)
    columns = []
    for n, src in enumerate((scale_hbm, shift_hbm)):
        columns.append(pltpu.make_async_copy(src.at[:, pl.ds(begin, COLS)], block.at[n], sems.at[4 + 2 * n]))
        columns.append(pltpu.make_async_copy(src.at[:, blocks * COLS:], tail.at[n], sems.at[5 + 2 * n]))
    for load in columns:
        load.start()
    chan, lat = w1.shape[1], wi_in.shape[1]
    slot = lax.axis_index("tm")
    wi_rows[...] = jnp.zeros_like(wi_rows)
    wo_rows[...] = jnp.zeros_like(wo_rows)
    for load in loads[1:3]:
        load.wait()
    for t in range(9):
        wi_rows[t * lat:(t + 1) * lat, :chan] = wi_in[t].astype(F32)
        wo_rows[t * TAP_ROWS:t * TAP_ROWS + lat] = wo_in[t].astype(F32)
    wi_ref[...] = jnp.transpose(wi_rows[...])[:chan].astype(BF)
    wo_ref[...] = wo_rows[...].astype(BF)
    for n, (w, u) in enumerate(((w1, u1), (w2, u2))):
        for dc, work in enumerate(weight_pieces(w, u)):
            for load in taps[n, dc]:
                load.wait()
            work()
    for load in loads[3:] + columns:
        load.wait()
    write_factors(factors, owner_ref, steps_ref, table_ref, slot, slots)
    for n, (dst, add) in enumerate(((scale_ref, 1.0), (shift_ref, 0.0))):
        column = None
        for ref, first in ((block, begin), (tail, blocks * COLS)):
            chosen = lax.broadcasted_iota(jnp.int32, ref.shape[1:], 1) + first == t_step
            part = jnp.sum(jnp.where(chosen, ref[n], 0.0), axis=1, keepdims=True)
            column = part if column is None else column + part
        dst[...] = jnp.broadcast_to(0.5 * (column + add), dst.shape)


def prep_call(slots, chan, scalars, given):
    V = pltpu.VMEM
    padded = (chan + COLS - 1) // COLS * COLS
    stay = lambda a: pltpu.with_memory_space_constraint(a, pltpu.HBM)
    scale, shift, wi, wo, w1, w2 = given
    return pl.pallas_call(
        functools.partial(prep_kernel, slots),
        out_shape=[V((chan, COLS), F32), V((chan, COLS), F32), V((chan, COLS), BF), V((9 * TAP_ROWS, chan), BF),
                   V((2 * slots + 3, 8, COLS), F32), V((4, chan, 3 * chan), BF), V((4, chan, 3 * chan), BF)],
        in_specs=[SMEM_SPEC] + [pl.BlockSpec(memory_space=pltpu.HBM)] * 8,
        out_specs=[VMEM_SPEC] * 7,
        scratch_shapes=[pltpu.SMEM(scalars[1].shape, jnp.int32), pltpu.SMEM(scalars[2].shape, F32), V(w1.shape, BF),
                        V(w2.shape, BF), V((2, chan, COLS), F32), V((2, chan, scale.shape[1] % COLS), F32), V(wi.shape, BF),
                        V(wo.shape, BF), V((COLS, padded), F32), V((9 * TAP_ROWS, chan), F32),
                        pltpu.SemaphoreType.DMA((28,))],
        compiler_params=pltpu.CompilerParams(vmem_limit_bytes=16 << 20),
        cost_estimate=pl.CostEstimate(flops=1 << 20, transcendentals=0, bytes_accessed=8 << 20),
        name="prep",
    )(scalars[0], *(stay(a) for a in scalars[1:]), *(stay(a) for a in given))


def drift_kernel(first, last, copies, slots, spaces, rows, sent_one, sent_two, got_one, got_two, *refs):
    if not first:
        sent_ref, *refs = refs
    (*kept, out_ref), refs = refs[:8], refs[8:]
    scale_ref, shift_ref, wi_ref, wo_ref, factors, u1, u2 = kept
    state, cols_in, keep, row_a, row_b, act_a, act_b, taps_out, prods = refs
    chan = scale_ref.shape[0]
    whole = chan // 256 * 256
    lat = out_ref.shape[-2]
    device_slot, space = lax.axis_index("tm"), lax.axis_index("space")
    lane = lax.broadcasted_iota(jnp.int32, (chan, COLS), 1)

    def masked(v, row):
        if 0 <= row < rows:
            return v
        at = space * rows + row
        return v * jnp.where((at >= 0) & (at < spaces * rows), 1.0, 0.0).astype(F32)

    own_rows = start_rows(space, got_two, got_one) + start_rows(space, sent_two, sent_one)
    own_rows += start_rows(space, sent_one, sent_two) + start_rows(space, got_one, got_two)
    for k, own in enumerate(own_rows):
        value = own
        if not first:
            row = k - HALO
            source = space
            if row < 0:
                source = jnp.maximum(space - 1, 0)
            elif row >= rows:
                source = jnp.minimum(space + 1, spaces - 1)
            at = slice(row % rows * COLS, (row % rows + 1) * COLS)
            total = None
            for q in range(slots):
                term = factors[q, :lat] * sent_ref[q, source, :, at].astype(F32)
                total = term if total is None else total + term
            value = masked(total, row) + factors[2 * slots, :lat] * own
        state[:, k * COLS:(k + 1) * COLS] = value.astype(BF).astype(F32)

    n_in = rows + 6
    cols_in[...] = jnp.zeros_like(cols_in)
    lane4 = lax.broadcasted_iota(jnp.int32, (lat, COLS), 1)
    for r in range(rows + 2 * HALO):
        x = state[:, r * COLS:(r + 1) * COLS]
        shifted = (
            jnp.where(lane4 == 0, 0.0, pltpu.roll(x, 1, 1)),
            x,
            jnp.where(lane4 == COLS - 1, 0.0, pltpu.roll(x, COLS - 1, 1)),
        )
        for dr in range(3):
            if 0 <= r - dr < n_in:
                for dc in range(3):
                    k = (3 * dr + dc) * lat
                    cols_in[k:k + lat, (r - dr) * COLS:(r - dr + 1) * COLS] = shifted[dc]
    wi = wi_ref[:, :cols_in.shape[0]]

    def transformed(src, dst, p):
        r0, r1, r2, r3 = (src[2 * p + k] for k in range(4))
        for i, v in enumerate((r0 - r2, r1 + r2, r2 - r1, r1 - r3)):
            v = v.astype(BF)
            zero = jnp.zeros_like(v)
            dst[p, i, 1] = v
            dst[p, i, 0] = jnp.where(lane == 0, zero, pltpu.roll(v, 1, 1))
            dst[p, i, 2] = jnp.where(lane == COLS - 1, zero, pltpu.roll(v, COLS - 1, 1))

    def first_layer(j):
        x = cols_in[:, j * 256:(j + 1) * 256].astype(BF)
        z = jnp.dot(wi, x, preferred_element_type=F32).astype(BF)
        for h in range(2):
            zh = z[:, h * COLS:(h + 1) * COLS]
            row = 2 * j + h
            keep[row] = zh
            row_a[row] = masked(silu(0.5 * zh.astype(F32)), row - 3)
        if j:
            transformed(row_a, act_a, j - 1)

    def product(src, u, pairs, i):
        chunks = []
        for lo, hi in ((0, whole), (whole, chan)):
            for dc in range(3):
                chunks.append(jnp.concatenate([src[p, i, dc, lo:hi] for p in pairs], axis=1))
        return jnp.dot(u[i], jnp.concatenate(chunks, axis=0), preferred_element_type=F32)

    def conv(src, u, pairs, beside, slot):
        for i in range(4):
            prods[slot, i, :, :COLS * len(pairs)] = product(src, u, pairs, i)
            for work in beside[i * len(beside) // 4:(i + 1) * len(beside) // 4]:
                work()

    def untransformed(slot, row):
        at = slice(row // 2 * COLS, (row // 2 + 1) * COLS)
        if row % 2 == 0:
            return prods[slot, 0, :, at] + prods[slot, 1, :, at] + prods[slot, 2, :, at]
        return prods[slot, 1, :, at] - prods[slot, 2, :, at] - prods[slot, 3, :, at]

    def finish_one(row, slot, n):
        y = untransformed(slot, n)
        row_b[row] = masked(silu(y * scale_ref[...] + shift_ref[...]), row - 2)
        if row >= 3 and row % 2:
            transformed(row_b, act_b, (row - 3) // 2)

    acts = {}

    def finish_two(row, slot, n):
        y = untransformed(slot, n)
        second = (keep[row + 2].astype(F32) + y).astype(BF).astype(F32)
        acts[row] = masked(silu(0.5 * second), row - 1).astype(BF)
        if row % 2:
            both = jnp.concatenate([acts.pop(row - 1), acts.pop(row)], axis=1)
            taps_out[row // 2] = jnp.dot(wo_ref[...], both, preferred_element_type=F32)

    pairs_one, pairs_two = (rows + 4) // 2, (rows + 2) // 2
    steps_one = [tuple(range(p, min(p + 2, pairs_one))) for p in range(0, pairs_one, 2)]
    steps_two = [tuple(range(p, min(p + 2, pairs_two))) for p in range(0, pairs_two, 2)]
    ready, slot = 0, 0
    waiting = []
    for pairs in steps_one:
        while ready <= pairs[-1] + 1:
            first_layer(ready)
            ready += 1
        beside = list(waiting)
        for j in range(ready, min(pairs[-1] + 4, pairs_one + 1)):
            beside.append(functools.partial(first_layer, j))
            ready = j + 1
        conv(act_a, u1, pairs, beside, slot)
        waiting = [functools.partial(finish_one, 2 * pairs[0] + n, slot, n) for n in range(2 * len(pairs))]
        slot = 1 - slot
    done = 2 * steps_one[-1][0]
    for pairs in steps_two:
        if 2 * pairs[-1] + 3 >= done:
            for work in waiting:
                work()
            waiting, done = [], 2 * pairs_one
        conv(act_b, u2, pairs, waiting, slot)
        done = 2 * pairs_one
        waiting = [functools.partial(finish_two, 2 * pairs[0] + n, slot, n) for n in range(2 * len(pairs))]
        slot = 1 - slot
    for work in waiting:
        work()

    lane8 = lax.broadcasted_iota(jnp.int32, (TAP_ROWS, COLS), 1)
    for r in range(rows):
        total = None
        for dc in range(3):
            v = None
            for dr in range(3):
                t = 3 * dr + dc
                q = r + dr
                p = taps_out[q // 2, TAP_ROWS * t:TAP_ROWS * (t + 1), q % 2 * COLS:(q % 2 + 1) * COLS]
                v = p if v is None else v + p
            if dc == 0:
                v = jnp.where(lane8 == 0, 0.0, pltpu.roll(v, 1, 1))
            elif dc == 2:
                v = jnp.where(lane8 == COLS - 1, 0.0, pltpu.roll(v, COLS - 1, 1))
            total = v if total is None else total + v
        drift = total[:lat].astype(BF).astype(F32)
        at = slice(r * COLS, (r + 1) * COLS)
        value = factors[2 * slots + 1, :lat] * drift + factors[2 * slots + 2, :lat] * own_rows[HALO + r]
        high = value.astype(BF)
        if last:
            low = (value - high.astype(F32)).astype(BF)
        for n in range(copies):
            if last:
                out_ref[n, 0, :, at] = high
                out_ref[n, 1, :, at] = low
            else:
                out_ref[n, :, at] = high


def drift_call(first, last, copies, slots, spaces, rows, chan, lat, tensors):
    V = pltpu.VMEM
    out = jax.ShapeDtypeStruct((copies, 2, lat, rows * COLS) if last else (copies, lat, rows * COLS), BF)
    scratch = [
        V((lat, (rows + 8) * COLS), F32), V((48, (rows + 6) * COLS), F32), V((rows + 6, chan, COLS), BF),
        V((rows + 6, chan, COLS), F32), V((rows + 4, chan, COLS), F32), V(((rows + 4) // 2, 4, 3, chan, COLS), BF),
        V(((rows + 2) // 2, 4, 3, chan, COLS), BF), V(((rows + 2) // 2, 9 * TAP_ROWS, 2 * COLS), F32),
        V((2, 4, chan, 2 * COLS), F32),
    ]
    passes = 2 * chan * (3 * chan) * 2 * COLS * (rows + 4 + rows + 2)
    return pl.pallas_call(
        functools.partial(drift_kernel, first, last, copies, slots, spaces, rows),
        out_shape=out,
        in_specs=[VMEM_SPEC] * len(tensors),
        out_specs=VMEM_SPEC,
        scratch_shapes=scratch,
        compiler_params=pltpu.CompilerParams(vmem_limit_bytes=25 << 20),
        cost_estimate=pl.CostEstimate(flops=passes, transcendentals=36 * chan * COLS, bytes_accessed=6 << 20),
        name="drift",
    )(*tensors)


def finish_kernel(slots, sent_one, sent_two, sent_ref, factors, iterate_ref, end_ref):
    rows, lat = iterate_ref.shape[2], iterate_ref.shape[1]
    space = lax.axis_index("space")
    own_rows = start_rows(space, sent_two, sent_one) + start_rows(space, sent_one, sent_two)
    for r in range(rows):
        at = slice(r * COLS, (r + 1) * COLS)
        lower, every = factors[2 * slots, :lat] * own_rows[r], None
        for q in range(slots):
            value = sent_ref[q, 0, :, at].astype(F32) + sent_ref[q, 1, :, at].astype(F32)
            full = factors[slots + q, :lat] * value
            lower = lower + factors[q, :lat] * value
            every = full if every is None else every + full
        iterate_ref[0, :, r, :] = lower
        end_ref[:, r, :] = every


def neighbour_rows(rows):
    count, index = lax.axis_size("space"), lax.axis_index("space")
    even = index % 2 == 0
    head, tail = rows[:, :HALO], rows[:, rows.shape[1] - HALO:]
    swap = lambda begin: [(i + a, i + 1 - a) for i in range(begin, count - 1, 2) for a in (0, 1)]
    one, two = jnp.where(even, tail, head), jnp.where(even, head, tail)
    return one, two, lax.ppermute(one, "space", swap(0)), lax.ppermute(two, "space", swap(1))


def body(latents, owner_slot, slot_steps, step_table, mod_scale, mod_shift, w_in, w_one, w_two, w_out):
    slots, spaces = lax.axis_size("tm"), lax.axis_size("space")
    lat, rows = latents.shape[1], latents.shape[2]
    assert rows == 2 * HALO
    state = neighbour_rows(latents[0])
    call = functools.partial(drift_call, slots=slots, spaces=spaces, rows=rows, chan=w_one.shape[1], lat=lat)
    everyone = slots * spaces
    weights = prep_call(slots, w_one.shape[1], (owner_slot, slot_steps, step_table), (
        mod_scale.T, mod_shift.T, jnp.transpose(w_in, (0, 2, 1)), w_out, w_one, w_two))
    drift = call(True, False, everyone, tensors=(*state, *weights))
    for picard_step in range(1, ITERS):
        last = picard_step == ITERS - 1
        sent = lax.all_to_all(drift, ("tm", "space"), 0, 0).reshape(slots, spaces, lat, rows * COLS)
        drift = call(False, last, slots if last else everyone, tensors=(*state, sent, *weights))
    sent = lax.all_to_all(drift, "tm", 0, 0)
    return pl.pallas_call(
        functools.partial(finish_kernel, slots),
        out_shape=(jax.ShapeDtypeStruct(latents.shape, F32), jax.ShapeDtypeStruct(latents.shape[1:], F32)),
        in_specs=[VMEM_SPEC] * 4,
        out_specs=(VMEM_SPEC, VMEM_SPEC),
        compiler_params=pltpu.CompilerParams(vmem_limit_bytes=4 << 20),
        name="finish",
    )(*state[:2], sent, weights[4])


def solution(mesh):
    in_specs = (P("tm", None, "space", None), P(), P(), P(), P(), P(), P(), P(), P(), P())
    out_specs = (P("tm", None, "space", None), P(None, "space", None))
    return jax.shard_map(body, mesh=mesh, in_specs=in_specs, out_specs=out_specs, check_vma=False)
```

```python
import functools

import jax
import jax.numpy as jnp
from jax import lax
from jax.experimental import pallas as pl
from jax.experimental.pallas import tpu as pltpu
from jax.sharding import PartitionSpec as P

ITERS = 3
HALO = 4
COLS = 128
TAP_ROWS = 8
F32, BF = jnp.float32, jnp.bfloat16
VMEM_SPEC = pl.BlockSpec(memory_space=pltpu.VMEM)
SMEM_SPEC = pl.BlockSpec(memory_space=pltpu.SMEM)


def silu(half):
    return half + half * jnp.tanh(half)


def position(slot, owner, slots):
    return lax.rem(slot - owner + slots, slots)


def write_factors(out, owner_ref, steps_ref, table_ref, slot, slots):
    owner = owner_ref[0]
    mine = position(slot, owner, slots)
    owns = slot == owner
    values = []
    for q in range(slots):
        size = table_ref[steps_ref[q]]
        below = jnp.where(position(q, owner, slots) < mine, size, 0.0)
        values.append(jnp.where(owns, 0.0, jnp.where(owner == q, 1.0, below)))
    values += [jnp.where(owner == q, 1.0, table_ref[steps_ref[q]]) for q in range(slots)]
    one = jnp.where(owns, 1.0, 0.0)
    values += [one, jnp.where(owns, table_ref[steps_ref[slot]], 1.0), one]
    for n, value in enumerate(values):
        out[n] = jnp.full(out.shape[1:], value, F32)


def start_rows(space, if_even, if_odd):
    return [jnp.where(lax.rem(space, 2) == 0, if_even[:, k], if_odd[:, k]) for k in range(HALO)]


def weight_pieces(w, u):
    whole = w.shape[1] // 256 * 256
    rest = {}

    def piece(dc):
        top, mid, low = (w[3 * dr + dc].astype(F32) for dr in range(3))
        even, odd = 0.5 * (top + low), 0.5 * mid
        for i, v in enumerate((w[dc], (even + odd).astype(BF), (even - odd).astype(BF), w[6 + dc])):
            u[i, :, dc * whole:(dc + 1) * whole] = v[:, :whole]
            rest[i, dc] = v[:, whole:]
        if dc == 2:
            for i in range(4):
                u[i, :, 3 * whole:] = jnp.concatenate([rest[i, k] for k in range(3)], axis=1)

    return [functools.partial(piece, dc) for dc in range(3)]


def prep_kernel(slots, owner_ref, steps_hbm, table_hbm, scale_hbm, shift_hbm, wi_hbm, wo_hbm, w1_hbm, w2_hbm,
                scale_ref, shift_ref, wi_ref, wo_ref, factors, u1, u2, steps_ref, table_ref, w1, w2, block, tail,
                wi_in, wo_in, wi_rows, wo_rows, sems):
    loads = [pltpu.make_async_copy(src, dst, sems.at[n]) for n, (src, dst) in enumerate(
        ((steps_hbm, steps_ref), (wi_hbm, wi_in), (wo_hbm, wo_in), (table_hbm, table_ref)))]
    taps = {(n, dc): [pltpu.make_async_copy(src.at[3 * dr + dc], dst.at[3 * dr + dc], sems.at[10 + 9 * n + 3 * dc + dr])
                      for dr in range(3)] for n, (src, dst) in enumerate(((w1_hbm, w1), (w2_hbm, w2))) for dc in range(3)}
    for load in loads + sum(taps.values(), []):
        load.start()
    blocks = scale_hbm.shape[1] // COLS
    loads[0].wait()
    t_step = steps_ref[lax.axis_index("tm")]
    begin = pl.multiple_of(jnp.minimum(t_step // COLS, blocks - 1) * COLS, COLS)
    columns = []
    for n, src in enumerate((scale_hbm, shift_hbm)):
        columns.append(pltpu.make_async_copy(src.at[:, pl.ds(begin, COLS)], block.at[n], sems.at[4 + 2 * n]))
        columns.append(pltpu.make_async_copy(src.at[:, blocks * COLS:], tail.at[n], sems.at[5 + 2 * n]))
    for load in columns:
        load.start()
    chan, lat = w1.shape[1], wi_in.shape[1]
    slot = lax.axis_index("tm")
    wi_rows[...] = jnp.zeros_like(wi_rows)
    wo_rows[...] = jnp.zeros_like(wo_rows)
    for load in loads[1:3]:
        load.wait()
    for t in range(9):
        wi_rows[t * lat:(t + 1) * lat, :chan] = wi_in[t].astype(F32)
        wo_rows[t * TAP_ROWS:t * TAP_ROWS + lat] = wo_in[t].astype(F32)
    wi_ref[...] = jnp.transpose(wi_rows[...])[:chan].astype(BF)
    wo_ref[...] = wo_rows[...].astype(BF)
    for n, (w, u) in enumerate(((w1, u1), (w2, u2))):
        for dc, work in enumerate(weight_pieces(w, u)):
            for load in taps[n, dc]:
                load.wait()
            work()
    for load in loads[3:] + columns:
        load.wait()
    write_factors(factors, owner_ref, steps_ref, table_ref, slot, slots)
    for n, (dst, add) in enumerate(((scale_ref, 1.0), (shift_ref, 0.0))):
        column = None
        for ref, first in ((block, begin), (tail, blocks * COLS)):
            chosen = lax.broadcasted_iota(jnp.int32, ref.shape[1:], 1) + first == t_step
            part = jnp.sum(jnp.where(chosen, ref[n], 0.0), axis=1, keepdims=True)
            column = part if column is None else column + part
        dst[...] = jnp.broadcast_to(0.5 * (column + add), dst.shape)


def prep_call(slots, chan, scalars, given):
    V = pltpu.VMEM
    padded = (chan + COLS - 1) // COLS * COLS
    stay = lambda a: pltpu.with_memory_space_constraint(a, pltpu.HBM)
    scale, shift, wi, wo, w1, w2 = given
    return pl.pallas_call(
        functools.partial(prep_kernel, slots),
        out_shape=[V((chan, COLS), F32), V((chan, COLS), F32), V((chan, COLS), BF), V((9 * TAP_ROWS, chan), BF),
                   V((2 * slots + 3, 8, COLS), F32), V((4, chan, 3 * chan), BF), V((4, chan, 3 * chan), BF)],
        in_specs=[SMEM_SPEC] + [pl.BlockSpec(memory_space=pltpu.HBM)] * 8,
        out_specs=[VMEM_SPEC] * 7,
        scratch_shapes=[pltpu.SMEM(scalars[1].shape, jnp.int32), pltpu.SMEM(scalars[2].shape, F32), V(w1.shape, BF),
                        V(w2.shape, BF), V((2, chan, COLS), F32), V((2, chan, scale.shape[1] % COLS), F32), V(wi.shape, BF),
                        V(wo.shape, BF), V((COLS, padded), F32), V((9 * TAP_ROWS, chan), F32),
                        pltpu.SemaphoreType.DMA((28,))],
        compiler_params=pltpu.CompilerParams(vmem_limit_bytes=16 << 20),
        cost_estimate=pl.CostEstimate(flops=1 << 20, transcendentals=0, bytes_accessed=8 << 20),
        name="prep",
    )(scalars[0], *(stay(a) for a in scalars[1:]), *(stay(a) for a in given))


def drift_kernel(first, last, copies, slots, spaces, rows, sent_one, sent_two, got_one, got_two, *refs):
    if not first:
        sent_ref, other_ref, *refs = refs
    (*kept, out_ref), refs = refs[:8], refs[8:]
    scale_ref, shift_ref, wi_ref, wo_ref, factors, u1, u2 = kept
    state, cols_in, keep, row_a, row_b, act_a, act_b, taps_out, prods = refs
    chan = scale_ref.shape[0]
    whole = chan // 256 * 256
    lat = out_ref.shape[-2]
    device_slot, space = lax.axis_index("tm"), lax.axis_index("space")
    lane = lax.broadcasted_iota(jnp.int32, (chan, COLS), 1)

    def masked(v, row):
        if 0 <= row < rows:
            return v
        at = space * rows + row
        return v * jnp.where((at >= 0) & (at < spaces * rows), 1.0, 0.0).astype(F32)

    own_rows = start_rows(space, got_two, got_one) + start_rows(space, sent_two, sent_one)
    own_rows += start_rows(space, sent_one, sent_two) + start_rows(space, got_one, got_two)
    first_core = lax.rem(device_slot, 2) == 0

    def weighed(ref, row):
        total = None
        for q in range(slots):
            term = factors[q, :lat] * ref[q, :, row * COLS:(row + 1) * COLS].astype(F32)
            total = term if total is None else total + term
        return total

    for k, own in enumerate(own_rows):
        value = own
        if not first:
            row = k - HALO
            if row < 0:
                total = masked(weighed(sent_ref.at[jnp.maximum(space - 1, 0)], k), row)
            elif row >= rows:
                total = masked(weighed(sent_ref.at[jnp.minimum(space + 1, spaces - 1)], row - rows), row)
            else:
                here, there = weighed(sent_ref.at[space], row % HALO), weighed(other_ref, row % HALO)
                total = jnp.where(first_core == (row < HALO), here, there)
            value = total + factors[2 * slots, :lat] * own
        state[:, k * COLS:(k + 1) * COLS] = value.astype(BF).astype(F32)

    n_in = rows + 6
    cols_in[...] = jnp.zeros_like(cols_in)
    lane4 = lax.broadcasted_iota(jnp.int32, (lat, COLS), 1)
    for r in range(rows + 2 * HALO):
        x = state[:, r * COLS:(r + 1) * COLS]
        shifted = (
            jnp.where(lane4 == 0, 0.0, pltpu.roll(x, 1, 1)),
            x,
            jnp.where(lane4 == COLS - 1, 0.0, pltpu.roll(x, COLS - 1, 1)),
        )
        for dr in range(3):
            if 0 <= r - dr < n_in:
                for dc in range(3):
                    k = (3 * dr + dc) * lat
                    cols_in[k:k + lat, (r - dr) * COLS:(r - dr + 1) * COLS] = shifted[dc]
    wi = wi_ref[:, :cols_in.shape[0]]

    def transformed(src, dst, p):
        r0, r1, r2, r3 = (src[2 * p + k] for k in range(4))
        for i, v in enumerate((r0 - r2, r1 + r2, r2 - r1, r1 - r3)):
            v = v.astype(BF)
            zero = jnp.zeros_like(v)
            dst[p, i, 1] = v
            dst[p, i, 0] = jnp.where(lane == 0, zero, pltpu.roll(v, 1, 1))
            dst[p, i, 2] = jnp.where(lane == COLS - 1, zero, pltpu.roll(v, COLS - 1, 1))

    def first_layer(j):
        x = cols_in[:, j * 256:(j + 1) * 256].astype(BF)
        z = jnp.dot(wi, x, preferred_element_type=F32).astype(BF)
        for h in range(2):
            zh = z[:, h * COLS:(h + 1) * COLS]
            row = 2 * j + h
            keep[row] = zh
            row_a[row] = masked(silu(0.5 * zh.astype(F32)), row - 3)
        if j:
            transformed(row_a, act_a, j - 1)

    def product(src, u, pairs, i):
        chunks = []
        for lo, hi in ((0, whole), (whole, chan)):
            for dc in range(3):
                chunks.append(jnp.concatenate([src[p, i, dc, lo:hi] for p in pairs], axis=1))
        return jnp.dot(u[i], jnp.concatenate(chunks, axis=0), preferred_element_type=F32)

    def conv(src, u, pairs, beside, slot):
        for i in range(4):
            prods[slot, i, :, :COLS * len(pairs)] = product(src, u, pairs, i)
            for work in beside[i * len(beside) // 4:(i + 1) * len(beside) // 4]:
                work()

    def untransformed(slot, row):
        at = slice(row // 2 * COLS, (row // 2 + 1) * COLS)
        if row % 2 == 0:
            return prods[slot, 0, :, at] + prods[slot, 1, :, at] + prods[slot, 2, :, at]
        return prods[slot, 1, :, at] - prods[slot, 2, :, at] - prods[slot, 3, :, at]

    def finish_one(row, slot, n):
        y = untransformed(slot, n)
        row_b[row] = masked(silu(y * scale_ref[...] + shift_ref[...]), row - 2)
        if row >= 3 and row % 2:
            transformed(row_b, act_b, (row - 3) // 2)

    acts = {}

    def finish_two(row, slot, n):
        y = untransformed(slot, n)
        second = (keep[row + 2].astype(F32) + y).astype(BF).astype(F32)
        acts[row] = masked(silu(0.5 * second), row - 1).astype(BF)
        if row % 2:
            both = jnp.concatenate([acts.pop(row - 1), acts.pop(row)], axis=1)
            taps_out[row // 2] = jnp.dot(wo_ref[...], both, preferred_element_type=F32)

    pairs_one, pairs_two = (rows + 4) // 2, (rows + 2) // 2
    steps_one = [tuple(range(p, min(p + 2, pairs_one))) for p in range(0, pairs_one, 2)]
    steps_two = [tuple(range(p, min(p + 2, pairs_two))) for p in range(0, pairs_two, 2)]
    ready, slot = 0, 0
    waiting = []
    for pairs in steps_one:
        while ready <= pairs[-1] + 1:
            first_layer(ready)
            ready += 1
        beside = list(waiting)
        for j in range(ready, min(pairs[-1] + 4, pairs_one + 1)):
            beside.append(functools.partial(first_layer, j))
            ready = j + 1
        conv(act_a, u1, pairs, beside, slot)
        waiting = [functools.partial(finish_one, 2 * pairs[0] + n, slot, n) for n in range(2 * len(pairs))]
        slot = 1 - slot
    done = 2 * steps_one[-1][0]
    for pairs in steps_two:
        if 2 * pairs[-1] + 3 >= done:
            for work in waiting:
                work()
            waiting, done = [], 2 * pairs_one
        conv(act_b, u2, pairs, waiting, slot)
        done = 2 * pairs_one
        waiting = [functools.partial(finish_two, 2 * pairs[0] + n, slot, n) for n in range(2 * len(pairs))]
        slot = 1 - slot
    for work in waiting:
        work()

    highs = []
    lane8 = lax.broadcasted_iota(jnp.int32, (TAP_ROWS, COLS), 1)
    for r in range(rows):
        total = None
        for dc in range(3):
            v = None
            for dr in range(3):
                t = 3 * dr + dc
                q = r + dr
                p = taps_out[q // 2, TAP_ROWS * t:TAP_ROWS * (t + 1), q % 2 * COLS:(q % 2 + 1) * COLS]
                v = p if v is None else v + p
            if dc == 0:
                v = jnp.where(lane8 == 0, 0.0, pltpu.roll(v, 1, 1))
            elif dc == 2:
                v = jnp.where(lane8 == COLS - 1, 0.0, pltpu.roll(v, COLS - 1, 1))
            total = v if total is None else total + v
        drift = total[:lat].astype(BF).astype(F32)
        at = slice(r * COLS, (r + 1) * COLS)
        value = factors[2 * slots + 1, :lat] * drift + factors[2 * slots + 2, :lat] * own_rows[HALO + r]
        high = value.astype(BF)
        highs.append(high)
        if last:
            low = (value - high.astype(F32)).astype(BF)
            for n in range(copies):
                out_ref[n, 0, :, at] = high
                out_ref[n, 1, :, at] = low
    if not last:
        for i in range(HALO):
            at = slice(i * COLS, (i + 1) * COLS)
            for k in range(spaces):
                to_first = jnp.where(k <= space, highs[i], highs[HALO + i])
                to_second = jnp.where(k < space, highs[i], highs[HALO + i])
                for t in range(slots):
                    out_ref[k * slots + t, :, at] = to_second if t % 2 else to_first


def drift_call(first, last, copies, slots, spaces, rows, chan, lat, tensors):
    V = pltpu.VMEM
    out = jax.ShapeDtypeStruct((copies, 2, lat, rows * COLS) if last else (copies, lat, HALO * COLS), BF)
    scratch = [
        V((lat, (rows + 8) * COLS), F32), V((48, (rows + 6) * COLS), F32), V((rows + 6, chan, COLS), BF),
        V((rows + 6, chan, COLS), F32), V((rows + 4, chan, COLS), F32), V(((rows + 4) // 2, 4, 3, chan, COLS), BF),
        V(((rows + 2) // 2, 4, 3, chan, COLS), BF), V(((rows + 2) // 2, 9 * TAP_ROWS, 2 * COLS), F32),
        V((2, 4, chan, 2 * COLS), F32),
    ]
    passes = 2 * chan * (3 * chan) * 2 * COLS * (rows + 4 + rows + 2)
    return pl.pallas_call(
        functools.partial(drift_kernel, first, last, copies, slots, spaces, rows),
        out_shape=out,
        in_specs=[VMEM_SPEC] * len(tensors),
        out_specs=VMEM_SPEC,
        scratch_shapes=scratch,
        compiler_params=pltpu.CompilerParams(vmem_limit_bytes=25 << 20),
        cost_estimate=pl.CostEstimate(flops=passes, transcendentals=36 * chan * COLS, bytes_accessed=6 << 20),
        name="drift",
    )(*tensors)


def finish_kernel(slots, sent_one, sent_two, sent_ref, factors, iterate_ref, end_ref):
    rows, lat = iterate_ref.shape[2], iterate_ref.shape[1]
    space = lax.axis_index("space")
    own_rows = start_rows(space, sent_two, sent_one) + start_rows(space, sent_one, sent_two)
    for r in range(rows):
        at = slice(r * COLS, (r + 1) * COLS)
        lower, every = factors[2 * slots, :lat] * own_rows[r], None
        for q in range(slots):
            value = sent_ref[q, 0, :, at].astype(F32) + sent_ref[q, 1, :, at].astype(F32)
            full = factors[slots + q, :lat] * value
            lower = lower + factors[q, :lat] * value
            every = full if every is None else every + full
        iterate_ref[0, :, r, :] = lower
        end_ref[:, r, :] = every


def neighbour_rows(rows):
    count, index = lax.axis_size("space"), lax.axis_index("space")
    even = index % 2 == 0
    head, tail = rows[:, :HALO], rows[:, rows.shape[1] - HALO:]
    swap = lambda begin: [(i + a, i + 1 - a) for i in range(begin, count - 1, 2) for a in (0, 1)]
    one, two = jnp.where(even, tail, head), jnp.where(even, head, tail)
    return one, two, lax.ppermute(one, "space", swap(0)), lax.ppermute(two, "space", swap(1))


def body(latents, owner_slot, slot_steps, step_table, mod_scale, mod_shift, w_in, w_one, w_two, w_out):
    slots, spaces = lax.axis_size("tm"), lax.axis_size("space")
    lat, rows = latents.shape[1], latents.shape[2]
    assert rows == 2 * HALO
    state = neighbour_rows(latents[0])
    call = functools.partial(drift_call, slots=slots, spaces=spaces, rows=rows, chan=w_one.shape[1], lat=lat)
    everyone = slots * spaces
    weights = prep_call(slots, w_one.shape[1], (owner_slot, slot_steps, step_table), (
        mod_scale.T, mod_shift.T, jnp.transpose(w_in, (0, 2, 1)), w_out, w_one, w_two))
    drift = call(True, False, everyone, tensors=(*state, *weights))
    here = lax.axis_index("space").astype(jnp.uint32)
    for picard_step in range(1, ITERS):
        last = picard_step == ITERS - 1
        drift, here = lax.optimization_barrier((drift, here))
        sent = lax.all_to_all(drift, ("space", "tm"), 0, 0).reshape(spaces, slots, lat, HALO * COLS)
        half = lax.dynamic_index_in_dim(sent, here, 0, keepdims=False)
        sent = (sent, lax.ppermute(half, "tm", [(t, t ^ 1) for t in range(slots)]))
        drift = call(False, last, slots if last else everyone, tensors=(*state, *sent, *weights))
    sent = lax.all_to_all(drift, "tm", 0, 0)
    return pl.pallas_call(
        functools.partial(finish_kernel, slots),
        out_shape=(jax.ShapeDtypeStruct(latents.shape, F32), jax.ShapeDtypeStruct(latents.shape[1:], F32)),
        in_specs=[VMEM_SPEC] * 4,
        out_specs=(VMEM_SPEC, VMEM_SPEC),
        compiler_params=pltpu.CompilerParams(vmem_limit_bytes=4 << 20),
        name="finish",
    )(*state[:2], sent, weights[4])


def solution(mesh):
    in_specs = (P("tm", None, "space", None), P(), P(), P(), P(), P(), P(), P(), P(), P())
    out_specs = (P("tm", None, "space", None), P(None, "space", None))
    return jax.shard_map(body, mesh=mesh, in_specs=in_specs, out_specs=out_specs, check_vma=False)
```

```python
import functools

import jax
import jax.numpy as jnp
from jax import lax
from jax.experimental import pallas as pl
from jax.experimental.pallas import tpu as pltpu
from jax.sharding import PartitionSpec as P

ITERS = 3
HALO = 4
COLS = 128
TAP_ROWS = 8
F32, BF = jnp.float32, jnp.bfloat16
VMEM_SPEC = pl.BlockSpec(memory_space=pltpu.VMEM)
SMEM_SPEC = pl.BlockSpec(memory_space=pltpu.SMEM)


def silu(half):
    return half + half * jnp.tanh(half)


def position(slot, owner, slots):
    return lax.rem(slot - owner + slots, slots)


def write_factors(out, owner_ref, steps_ref, table_ref, slot, slots):
    owner = owner_ref[0]
    mine = position(slot, owner, slots)
    owns = slot == owner
    values = []
    for q in range(slots):
        size = table_ref[steps_ref[q]]
        below = jnp.where(position(q, owner, slots) < mine, size, 0.0)
        values.append(jnp.where(owns, 0.0, jnp.where(owner == q, 1.0, below)))
    values += [jnp.where(owner == q, 1.0, table_ref[steps_ref[q]]) for q in range(slots)]
    one = jnp.where(owns, 1.0, 0.0)
    values += [one, jnp.where(owns, table_ref[steps_ref[slot]], 1.0), one]
    for n, value in enumerate(values):
        out[n] = jnp.full(out.shape[1:], value, F32)


def start_rows(space, if_even, if_odd):
    return [jnp.where(lax.rem(space, 2) == 0, if_even[:, k], if_odd[:, k]) for k in range(HALO)]


def weight_pieces(w, u):
    whole = w.shape[1] // 256 * 256
    rest = {}

    def piece(dc):
        top, mid, low = (w[3 * dr + dc].astype(F32) for dr in range(3))
        even, odd = 0.5 * (top + low), 0.5 * mid
        for i, v in enumerate((w[dc], (even + odd).astype(BF), (even - odd).astype(BF), w[6 + dc])):
            u[i, :, dc * whole:(dc + 1) * whole] = v[:, :whole]
            rest[i, dc] = v[:, whole:]
        if dc == 2:
            for i in range(4):
                u[i, :, 3 * whole:] = jnp.concatenate([rest[i, k] for k in range(3)], axis=1)

    return [functools.partial(piece, dc) for dc in range(3)]


def prep_kernel(slots, owner_ref, steps_hbm, table_hbm, scale_hbm, shift_hbm, wi_hbm, wo_hbm, w1_hbm, w2_hbm,
                scale_ref, shift_ref, wi_ref, wo_ref, factors, u1, u2, steps_ref, table_ref, w1, w2, block, tail,
                wi_in, wo_in, wi_rows, wo_rows, sems):
    loads = [pltpu.make_async_copy(src, dst, sems.at[n]) for n, (src, dst) in enumerate(
        ((steps_hbm, steps_ref), (wi_hbm, wi_in), (wo_hbm, wo_in), (table_hbm, table_ref)))]
    taps = {(n, dc): [pltpu.make_async_copy(src.at[3 * dr + dc], dst.at[3 * dr + dc], sems.at[10 + 9 * n + 3 * dc + dr])
                      for dr in range(3)] for n, (src, dst) in enumerate(((w1_hbm, w1), (w2_hbm, w2))) for dc in range(3)}
    for load in loads + sum(taps.values(), [])[:9]:
        load.start()
    blocks = scale_hbm.shape[1] // COLS
    loads[0].wait()
    t_step = steps_ref[lax.axis_index("tm")]
    begin = pl.multiple_of(jnp.minimum(t_step // COLS, blocks - 1) * COLS, COLS)
    columns = []
    for n, src in enumerate((scale_hbm, shift_hbm)):
        columns.append(pltpu.make_async_copy(src.at[:, pl.ds(begin, COLS)], block.at[n], sems.at[4 + 2 * n]))
        columns.append(pltpu.make_async_copy(src.at[:, blocks * COLS:], tail.at[n], sems.at[5 + 2 * n]))
    for load in columns + sum(taps.values(), [])[9:]:
        load.start()
    chan, lat = w1.shape[1], wi_in.shape[1]
    slot = lax.axis_index("tm")
    wi_rows[...] = jnp.zeros_like(wi_rows)
    wo_rows[...] = jnp.zeros_like(wo_rows)
    for load in loads[1:3]:
        load.wait()
    for t in range(9):
        wi_rows[t * lat:(t + 1) * lat, :chan] = wi_in[t].astype(F32)
        wo_rows[t * TAP_ROWS:t * TAP_ROWS + lat] = wo_in[t].astype(F32)
    wi_ref[...] = jnp.transpose(wi_rows[...])[:chan].astype(BF)
    wo_ref[...] = wo_rows[...].astype(BF)

    def transform(n, w, u):
        for dc, work in enumerate(weight_pieces(w, u)):
            for load in taps[n, dc]:
                load.wait()
            work()

    transform(0, w1, u1)
    for load in loads[3:] + columns:
        load.wait()
    write_factors(factors, owner_ref, steps_ref, table_ref, slot, slots)
    for n, (dst, add) in enumerate(((scale_ref, 1.0), (shift_ref, 0.0))):
        column = None
        for ref, first in ((block, begin), (tail, blocks * COLS)):
            chosen = lax.broadcasted_iota(jnp.int32, ref.shape[1:], 1) + first == t_step
            part = jnp.sum(jnp.where(chosen, ref[n], 0.0), axis=1, keepdims=True)
            column = part if column is None else column + part
        dst[...] = jnp.broadcast_to(0.5 * (column + add), dst.shape)
    transform(1, w2, u2)


def prep_call(slots, chan, scalars, given):
    V = pltpu.VMEM
    padded = (chan + COLS - 1) // COLS * COLS
    stay = lambda a: pltpu.with_memory_space_constraint(a, pltpu.HBM)
    scale, shift, wi, wo, w1, w2 = given
    return pl.pallas_call(
        functools.partial(prep_kernel, slots),
        out_shape=[V((chan, COLS), F32), V((chan, COLS), F32), V((chan, COLS), BF), V((9 * TAP_ROWS, chan), BF),
                   V((2 * slots + 3, 8, COLS), F32), V((4, chan, 3 * chan), BF), V((4, chan, 3 * chan), BF)],
        in_specs=[SMEM_SPEC] + [pl.BlockSpec(memory_space=pltpu.HBM)] * 8,
        out_specs=[VMEM_SPEC] * 7,
        scratch_shapes=[pltpu.SMEM(scalars[1].shape, jnp.int32), pltpu.SMEM(scalars[2].shape, F32), V(w1.shape, BF),
                        V(w2.shape, BF), V((2, chan, COLS), F32), V((2, chan, scale.shape[1] % COLS), F32), V(wi.shape, BF),
                        V(wo.shape, BF), V((COLS, padded), F32), V((9 * TAP_ROWS, chan), F32),
                        pltpu.SemaphoreType.DMA((28,))],
        compiler_params=pltpu.CompilerParams(vmem_limit_bytes=16 << 20),
        cost_estimate=pl.CostEstimate(flops=1 << 20, transcendentals=0, bytes_accessed=8 << 20),
        name="prep",
    )(scalars[0], *(stay(a) for a in scalars[1:]), *(stay(a) for a in given))


def drift_kernel(first, last, copies, slots, spaces, rows, sent_one, sent_two, got_one, got_two, *refs):
    if not first:
        sent_ref, other_ref, *refs = refs
    (*kept, out_ref), refs = refs[:8], refs[8:]
    scale_ref, shift_ref, wi_ref, wo_ref, factors, u1, u2 = kept
    state, cols_in, keep, row_a, row_b, act_a, act_b, taps_out, prods = refs
    chan = scale_ref.shape[0]
    whole = chan // 256 * 256
    lat = out_ref.shape[-2]
    device_slot, space = lax.axis_index("tm"), lax.axis_index("space")
    lane = lax.broadcasted_iota(jnp.int32, (chan, COLS), 1)

    def masked(v, row):
        if 0 <= row < rows:
            return v
        at = space * rows + row
        return v * jnp.where((at >= 0) & (at < spaces * rows), 1.0, 0.0).astype(F32)

    own_rows = start_rows(space, got_two, got_one) + start_rows(space, sent_two, sent_one)
    own_rows += start_rows(space, sent_one, sent_two) + start_rows(space, got_one, got_two)
    first_core = lax.rem(device_slot, 2) == 0

    def weighed(ref, row):
        total = None
        for q in range(slots):
            term = factors[q, :lat] * ref[q, :, row * COLS:(row + 1) * COLS].astype(F32)
            total = term if total is None else total + term
        return total

    if not first:
        here = [weighed(sent_ref.at[space], i) for i in range(HALO)]
        there = [weighed(other_ref, i) for i in range(HALO)]
    for k, own in enumerate(own_rows):
        value = own
        if not first:
            row = k - HALO
            if row < 0:
                total = masked(weighed(sent_ref.at[jnp.maximum(space - 1, 0)], k), row)
            elif row >= rows:
                total = masked(weighed(sent_ref.at[jnp.minimum(space + 1, spaces - 1)], row - rows), row)
            else:
                total = jnp.where(first_core == (row < HALO), here[row % HALO], there[row % HALO])
            value = total + factors[2 * slots, :lat] * own
        state[:, k * COLS:(k + 1) * COLS] = value.astype(BF).astype(F32)

    n_in = rows + 6
    cols_in[...] = jnp.zeros_like(cols_in)
    lane4 = lax.broadcasted_iota(jnp.int32, (lat, COLS), 1)
    for r in range(rows + 2 * HALO):
        x = state[:, r * COLS:(r + 1) * COLS]
        shifted = (
            jnp.where(lane4 == 0, 0.0, pltpu.roll(x, 1, 1)),
            x,
            jnp.where(lane4 == COLS - 1, 0.0, pltpu.roll(x, COLS - 1, 1)),
        )
        for dr in range(3):
            if 0 <= r - dr < n_in:
                for dc in range(3):
                    k = (3 * dr + dc) * lat
                    cols_in[k:k + lat, (r - dr) * COLS:(r - dr + 1) * COLS] = shifted[dc]
    wi = wi_ref[:, :cols_in.shape[0]]

    def transformed(src, dst, p):
        r0, r1, r2, r3 = (src[2 * p + k] for k in range(4))
        for i, v in enumerate((r0 - r2, r1 + r2, r2 - r1, r1 - r3)):
            v = v.astype(BF)
            zero = jnp.zeros_like(v)
            dst[p, i, 1] = v
            dst[p, i, 0] = jnp.where(lane == 0, zero, pltpu.roll(v, 1, 1))
            dst[p, i, 2] = jnp.where(lane == COLS - 1, zero, pltpu.roll(v, COLS - 1, 1))

    def first_layer(j):
        x = cols_in[:, j * 256:(j + 1) * 256].astype(BF)
        z = jnp.dot(wi, x, preferred_element_type=F32).astype(BF)
        for h in range(2):
            zh = z[:, h * COLS:(h + 1) * COLS]
            row = 2 * j + h
            keep[row] = zh
            row_a[row] = masked(silu(0.5 * zh.astype(F32)), row - 3)
        if j:
            transformed(row_a, act_a, j - 1)

    def product(src, u, pairs, i):
        chunks = []
        for lo, hi in ((0, whole), (whole, chan)):
            for dc in range(3):
                chunks.append(jnp.concatenate([src[p, i, dc, lo:hi] for p in pairs], axis=1))
        return jnp.dot(u[i], jnp.concatenate(chunks, axis=0), preferred_element_type=F32)

    def conv(src, u, pairs, beside, slot):
        for i in range(4):
            prods[slot, i, :, :COLS * len(pairs)] = product(src, u, pairs, i)
            for work in beside[i * len(beside) // 4:(i + 1) * len(beside) // 4]:
                work()

    def untransformed(slot, row):
        at = slice(row // 2 * COLS, (row // 2 + 1) * COLS)
        if row % 2 == 0:
            return prods[slot, 0, :, at] + prods[slot, 1, :, at] + prods[slot, 2, :, at]
        return prods[slot, 1, :, at] - prods[slot, 2, :, at] - prods[slot, 3, :, at]

    def finish_one(row, slot, n):
        y = untransformed(slot, n)
        row_b[row] = masked(silu(y * scale_ref[...] + shift_ref[...]), row - 2)
        if row >= 3 and row % 2:
            transformed(row_b, act_b, (row - 3) // 2)

    acts = {}

    def finish_two(row, slot, n):
        y = untransformed(slot, n)
        second = (keep[row + 2].astype(F32) + y).astype(BF).astype(F32)
        acts[row] = masked(silu(0.5 * second), row - 1).astype(BF)
        if row % 2:
            both = jnp.concatenate([acts.pop(row - 1), acts.pop(row)], axis=1)
            taps_out[row // 2] = jnp.dot(wo_ref[...], both, preferred_element_type=F32)

    pairs_one, pairs_two = (rows + 4) // 2, (rows + 2) // 2
    steps_one = [tuple(range(p, min(p + 2, pairs_one))) for p in range(0, pairs_one, 2)]
    steps_two = [tuple(range(p, min(p + 2, pairs_two))) for p in range(0, pairs_two, 2)]
    ready, slot = 0, 0
    waiting = []
    for pairs in steps_one:
        while ready <= pairs[-1] + 1:
            first_layer(ready)
            ready += 1
        beside = list(waiting)
        for j in range(ready, min(pairs[-1] + 4, pairs_one + 1)):
            beside.append(functools.partial(first_layer, j))
            ready = j + 1
        conv(act_a, u1, pairs, beside, slot)
        waiting = [functools.partial(finish_one, 2 * pairs[0] + n, slot, n) for n in range(2 * len(pairs))]
        slot = 1 - slot
    done = 2 * steps_one[-1][0]
    for pairs in steps_two:
        if 2 * pairs[-1] + 3 >= done:
            for work in waiting:
                work()
            waiting, done = [], 2 * pairs_one
        conv(act_b, u2, pairs, waiting, slot)
        done = 2 * pairs_one
        waiting = [functools.partial(finish_two, 2 * pairs[0] + n, slot, n) for n in range(2 * len(pairs))]
        slot = 1 - slot
    for work in waiting:
        work()

    highs = []
    lane8 = lax.broadcasted_iota(jnp.int32, (TAP_ROWS, COLS), 1)
    for r in range(rows):
        total = None
        for dc in range(3):
            v = None
            for dr in range(3):
                t = 3 * dr + dc
                q = r + dr
                p = taps_out[q // 2, TAP_ROWS * t:TAP_ROWS * (t + 1), q % 2 * COLS:(q % 2 + 1) * COLS]
                v = p if v is None else v + p
            if dc == 0:
                v = jnp.where(lane8 == 0, 0.0, pltpu.roll(v, 1, 1))
            elif dc == 2:
                v = jnp.where(lane8 == COLS - 1, 0.0, pltpu.roll(v, COLS - 1, 1))
            total = v if total is None else total + v
        drift = total[:lat].astype(BF).astype(F32)
        at = slice(r * COLS, (r + 1) * COLS)
        value = factors[2 * slots + 1, :lat] * drift + factors[2 * slots + 2, :lat] * own_rows[HALO + r]
        high = value.astype(BF)
        highs.append(high)
        if last:
            low = (value - high.astype(F32)).astype(BF)
            for n in range(copies):
                out_ref[n, 0, :, at] = high
                out_ref[n, 1, :, at] = low
    if not last:
        for i in range(HALO):
            at = slice(i * COLS, (i + 1) * COLS)
            for k in range(spaces):
                to_first = jnp.where(k <= space, highs[i], highs[HALO + i])
                to_second = jnp.where(k < space, highs[i], highs[HALO + i])
                for t in range(slots):
                    out_ref[k * slots + t, :, at] = to_second if t % 2 else to_first


def drift_call(first, last, copies, slots, spaces, rows, chan, lat, tensors):
    V = pltpu.VMEM
    out = jax.ShapeDtypeStruct((copies, 2, lat, rows * COLS) if last else (copies, lat, HALO * COLS), BF)
    scratch = [
        V((lat, (rows + 8) * COLS), F32), V((48, (rows + 6) * COLS), F32), V((rows + 6, chan, COLS), BF),
        V((rows + 6, chan, COLS), F32), V((rows + 4, chan, COLS), F32), V(((rows + 4) // 2, 4, 3, chan, COLS), BF),
        V(((rows + 2) // 2, 4, 3, chan, COLS), BF), V(((rows + 2) // 2, 9 * TAP_ROWS, 2 * COLS), F32),
        V((2, 4, chan, 2 * COLS), F32),
    ]
    passes = 2 * chan * (3 * chan) * 2 * COLS * (rows + 4 + rows + 2)
    return pl.pallas_call(
        functools.partial(drift_kernel, first, last, copies, slots, spaces, rows),
        out_shape=out,
        in_specs=[VMEM_SPEC] * len(tensors),
        out_specs=VMEM_SPEC,
        scratch_shapes=scratch,
        compiler_params=pltpu.CompilerParams(vmem_limit_bytes=25 << 20),
        cost_estimate=pl.CostEstimate(flops=passes, transcendentals=36 * chan * COLS, bytes_accessed=6 << 20),
        name="drift",
    )(*tensors)


def finish_kernel(slots, sent_one, sent_two, sent_ref, factors, iterate_ref, end_ref):
    rows, lat = iterate_ref.shape[2], iterate_ref.shape[1]
    space = lax.axis_index("space")
    own_rows = start_rows(space, sent_two, sent_one) + start_rows(space, sent_one, sent_two)
    for r in range(rows):
        at = slice(r * COLS, (r + 1) * COLS)
        lower, every = factors[2 * slots, :lat] * own_rows[r], None
        for q in range(slots):
            value = sent_ref[q, 0, :, at].astype(F32) + sent_ref[q, 1, :, at].astype(F32)
            full = factors[slots + q, :lat] * value
            lower = lower + factors[q, :lat] * value
            every = full if every is None else every + full
        iterate_ref[0, :, r, :] = lower
        end_ref[:, r, :] = every


def neighbour_rows(rows):
    count, index = lax.axis_size("space"), lax.axis_index("space")
    even = index % 2 == 0
    head, tail = rows[:, :HALO], rows[:, rows.shape[1] - HALO:]
    swap = lambda begin: [(i + a, i + 1 - a) for i in range(begin, count - 1, 2) for a in (0, 1)]
    one, two = jnp.where(even, tail, head), jnp.where(even, head, tail)
    return one, two, lax.ppermute(one, "space", swap(0)), lax.ppermute(two, "space", swap(1))


def body(latents, owner_slot, slot_steps, step_table, mod_scale, mod_shift, w_in, w_one, w_two, w_out):
    slots, spaces = lax.axis_size("tm"), lax.axis_size("space")
    lat, rows = latents.shape[1], latents.shape[2]
    assert rows == 2 * HALO
    state = neighbour_rows(latents[0])
    call = functools.partial(drift_call, slots=slots, spaces=spaces, rows=rows, chan=w_one.shape[1], lat=lat)
    everyone = slots * spaces
    weights = prep_call(slots, w_one.shape[1], (owner_slot, slot_steps, step_table), (
        mod_scale.T, mod_shift.T, jnp.transpose(w_in, (0, 2, 1)), w_out, w_one, w_two))
    drift = call(True, False, everyone, tensors=(*state, *weights))
    here = lax.axis_index("space").astype(jnp.uint32)
    for picard_step in range(1, ITERS):
        last = picard_step == ITERS - 1
        drift, here = lax.optimization_barrier((drift, here))
        sent = lax.all_to_all(drift, ("space", "tm"), 0, 0).reshape(spaces, slots, lat, HALO * COLS)
        half = lax.dynamic_index_in_dim(sent, here, 0, keepdims=False)
        sent = (sent, lax.ppermute(half, "tm", [(t, t ^ 1) for t in range(slots)]))
        drift = call(False, last, slots if last else everyone, tensors=(*state, *sent, *weights))
    sent = lax.all_to_all(drift, "tm", 0, 0)
    return pl.pallas_call(
        functools.partial(finish_kernel, slots),
        out_shape=(jax.ShapeDtypeStruct(latents.shape, F32), jax.ShapeDtypeStruct(latents.shape[1:], F32)),
        in_specs=[VMEM_SPEC] * 4,
        out_specs=(VMEM_SPEC, VMEM_SPEC),
        compiler_params=pltpu.CompilerParams(vmem_limit_bytes=4 << 20),
        name="finish",
    )(*state[:2], sent, weights[4])


def solution(mesh):
    in_specs = (P("tm", None, "space", None), P(), P(), P(), P(), P(), P(), P(), P(), P())
    out_specs = (P("tm", None, "space", None), P(None, "space", None))
    return jax.shard_map(body, mesh=mesh, in_specs=in_specs, out_specs=out_specs, check_vma=False)
```

```python
import functools

import jax
import jax.numpy as jnp
from jax import lax
from jax.experimental import pallas as pl
from jax.experimental.pallas import tpu as pltpu
from jax.sharding import PartitionSpec as P

ITERS = 3
HALO = 4
COLS = 128
TAP_ROWS = 8
F32, BF = jnp.float32, jnp.bfloat16
VMEM_SPEC = pl.BlockSpec(memory_space=pltpu.VMEM)
SMEM_SPEC = pl.BlockSpec(memory_space=pltpu.SMEM)


def silu(half):
    return half + half * jnp.tanh(half)


def position(slot, owner, slots):
    return lax.rem(slot - owner + slots, slots)


def write_factors(out, owner_ref, steps_ref, table_ref, slot, slots):
    owner = owner_ref[0]
    mine = position(slot, owner, slots)
    owns = slot == owner
    values = []
    for q in range(slots):
        size = table_ref[steps_ref[q]]
        below = jnp.where(position(q, owner, slots) < mine, size, 0.0)
        values.append(jnp.where(owns, 0.0, jnp.where(owner == q, 1.0, below)))
    values += [jnp.where(owner == q, 1.0, table_ref[steps_ref[q]]) for q in range(slots)]
    one = jnp.where(owns, 1.0, 0.0)
    values += [one, jnp.where(owns, table_ref[steps_ref[slot]], 1.0), one]
    for n, value in enumerate(values):
        out[n] = jnp.full(out.shape[1:], value, F32)


def start_rows(space, if_even, if_odd):
    return [jnp.where(lax.rem(space, 2) == 0, if_even[:, k], if_odd[:, k]) for k in range(HALO)]


def weight_pieces(w, u):
    whole = w.shape[1] // 256 * 256
    rest = {}

    def piece(dc):
        top, mid, low = (w[3 * dr + dc].astype(F32) for dr in range(3))
        even, odd = 0.5 * (top + low), 0.5 * mid
        for i, v in enumerate((w[dc], (even + odd).astype(BF), (even - odd).astype(BF), w[6 + dc])):
            u[i, :, dc * whole:(dc + 1) * whole] = v[:, :whole]
            rest[i, dc] = v[:, whole:]
        if dc == 2:
            for i in range(4):
                u[i, :, 3 * whole:] = jnp.concatenate([rest[i, k] for k in range(3)], axis=1)

    return [functools.partial(piece, dc) for dc in range(3)]


def prep_kernel(slots, owner_ref, steps_hbm, table_hbm, scale_hbm, shift_hbm, wi_hbm, wo_hbm, w1_hbm, w2_hbm,
                scale_ref, shift_ref, wi_ref, wo_ref, factors, u1, u2, steps_ref, table_ref, w1, w2, block, tail,
                wi_in, wo_in, wi_rows, wo_rows, sems):
    loads = [pltpu.make_async_copy(src, dst, sems.at[n]) for n, (src, dst) in enumerate(
        ((steps_hbm, steps_ref), (wi_hbm, wi_in), (wo_hbm, wo_in), (table_hbm, table_ref)))]
    taps = {(n, dc): [pltpu.make_async_copy(src.at[3 * dr + dc], dst.at[3 * dr + dc], sems.at[10 + 9 * n + 3 * dc + dr])
                      for dr in range(3)] for n, (src, dst) in enumerate(((w1_hbm, w1), (w2_hbm, w2))) for dc in range(3)}
    for load in loads + sum(taps.values(), [])[:9]:
        load.start()
    blocks = scale_hbm.shape[1] // COLS
    loads[0].wait()
    t_step = steps_ref[lax.axis_index("tm")]
    begin = pl.multiple_of(jnp.minimum(t_step // COLS, blocks - 1) * COLS, COLS)
    columns = []
    for n, src in enumerate((scale_hbm, shift_hbm)):
        columns.append(pltpu.make_async_copy(src.at[:, pl.ds(begin, COLS)], block.at[n], sems.at[4 + 2 * n]))
        columns.append(pltpu.make_async_copy(src.at[:, blocks * COLS:], tail.at[n], sems.at[5 + 2 * n]))
    for load in columns + sum(taps.values(), [])[9:]:
        load.start()
    chan, lat = w1.shape[1], wi_in.shape[1]
    slot = lax.axis_index("tm")
    wi_rows[...] = jnp.zeros_like(wi_rows)
    wo_rows[...] = jnp.zeros_like(wo_rows)
    for load in loads[1:3]:
        load.wait()
    for t in range(9):
        wi_rows[t * lat:(t + 1) * lat, :chan] = wi_in[t].astype(F32)
        wo_rows[t * TAP_ROWS:t * TAP_ROWS + lat] = wo_in[t].astype(F32)
    wi_ref[...] = jnp.transpose(wi_rows[...])[:chan].astype(BF)
    wo_ref[...] = wo_rows[...].astype(BF)

    def transform(n, w, u):
        for dc, work in enumerate(weight_pieces(w, u)):
            for load in taps[n, dc]:
                load.wait()
            work()

    transform(0, w1, u1)
    for load in loads[3:] + columns:
        load.wait()
    write_factors(factors, owner_ref, steps_ref, table_ref, slot, slots)
    for n, (dst, add) in enumerate(((scale_ref, 1.0), (shift_ref, 0.0))):
        column = None
        for ref, first in ((block, begin), (tail, blocks * COLS)):
            chosen = lax.broadcasted_iota(jnp.int32, ref.shape[1:], 1) + first == t_step
            part = jnp.sum(jnp.where(chosen, ref[n], 0.0), axis=1, keepdims=True)
            column = part if column is None else column + part
        dst[...] = jnp.broadcast_to(0.5 * (column + add), dst.shape)
    transform(1, w2, u2)


def prep_call(slots, chan, scalars, given):
    V = pltpu.VMEM
    padded = (chan + COLS - 1) // COLS * COLS
    stay = lambda a: pltpu.with_memory_space_constraint(a, pltpu.HBM)
    scale, shift, wi, wo, w1, w2 = given
    return pl.pallas_call(
        functools.partial(prep_kernel, slots),
        out_shape=[V((chan, COLS), F32), V((chan, COLS), F32), V((chan, COLS), BF), V((9 * TAP_ROWS, chan), BF),
                   V((2 * slots + 3, 8, COLS), F32), V((4, chan, 3 * chan), BF), V((4, chan, 3 * chan), BF)],
        in_specs=[SMEM_SPEC] + [pl.BlockSpec(memory_space=pltpu.HBM)] * 8,
        out_specs=[VMEM_SPEC] * 7,
        scratch_shapes=[pltpu.SMEM(scalars[1].shape, jnp.int32), pltpu.SMEM(scalars[2].shape, F32), V(w1.shape, BF),
                        V(w2.shape, BF), V((2, chan, COLS), F32), V((2, chan, scale.shape[1] % COLS), F32), V(wi.shape, BF),
                        V(wo.shape, BF), V((COLS, padded), F32), V((9 * TAP_ROWS, chan), F32),
                        pltpu.SemaphoreType.DMA((28,))],
        compiler_params=pltpu.CompilerParams(vmem_limit_bytes=16 << 20),
        cost_estimate=pl.CostEstimate(flops=1 << 20, transcendentals=0, bytes_accessed=8 << 20),
        name="prep",
    )(scalars[0], *(stay(a) for a in scalars[1:]), *(stay(a) for a in given))


def drift_kernel(first, last, copies, slots, spaces, rows, sent_one, sent_two, got_one, got_two, *refs):
    if not first:
        sent_ref, other_ref, *refs = refs
    (*kept, out_ref), refs = refs[:8], refs[8:]
    scale_ref, shift_ref, wi_ref, wo_ref, factors, u1, u2 = kept
    state, cols_in, keep, row_a, row_b, act_a, act_b, taps_out, prods = refs
    chan = scale_ref.shape[0]
    whole = chan // 256 * 256
    lat = out_ref.shape[-2]
    device_slot, space = lax.axis_index("tm"), lax.axis_index("space")
    lane = lax.broadcasted_iota(jnp.int32, (chan, COLS), 1)

    def masked(v, row):
        if 0 <= row < rows:
            return v
        at = space * rows + row
        return v * jnp.where((at >= 0) & (at < spaces * rows), 1.0, 0.0).astype(F32)

    own_rows = start_rows(space, got_two, got_one) + start_rows(space, sent_two, sent_one)
    own_rows += start_rows(space, sent_one, sent_two) + start_rows(space, got_one, got_two)
    first_core = lax.rem(device_slot, 2) == 0

    def weighed(ref, row):
        total = None
        for q in range(slots):
            term = factors[q, :lat] * ref[q, :, row * COLS:(row + 1) * COLS].astype(F32)
            total = term if total is None else total + term
        return total

    if not first:
        here = [weighed(sent_ref.at[space], i) for i in range(HALO)]
        there = [weighed(other_ref, i) for i in range(HALO)]
    for k, own in enumerate(own_rows):
        value = own
        if not first:
            row = k - HALO
            if row < 0:
                total = masked(weighed(sent_ref.at[jnp.maximum(space - 1, 0)], k), row)
            elif row >= rows:
                total = masked(weighed(sent_ref.at[jnp.minimum(space + 1, spaces - 1)], row - rows), row)
            else:
                total = jnp.where(first_core == (row < HALO), here[row % HALO], there[row % HALO])
            value = total + factors[2 * slots, :lat] * own
        state[:, k * COLS:(k + 1) * COLS] = value.astype(BF).astype(F32)

    n_in = rows + 6
    cols_in[...] = jnp.zeros_like(cols_in)
    lane4 = lax.broadcasted_iota(jnp.int32, (lat, COLS), 1)
    for r in range(rows + 2 * HALO):
        x = state[:, r * COLS:(r + 1) * COLS]
        shifted = (
            jnp.where(lane4 == 0, 0.0, pltpu.roll(x, 1, 1)),
            x,
            jnp.where(lane4 == COLS - 1, 0.0, pltpu.roll(x, COLS - 1, 1)),
        )
        for dr in range(3):
            if 0 <= r - dr < n_in:
                for dc in range(3):
                    k = (3 * dr + dc) * lat
                    cols_in[k:k + lat, (r - dr) * COLS:(r - dr + 1) * COLS] = shifted[dc]
    wi = wi_ref[:, :cols_in.shape[0]]

    def transformed(src, dst, p):
        r0, r1, r2, r3 = (src[2 * p + k] for k in range(4))
        for i, v in enumerate((r0 - r2, r1 + r2, r2 - r1, r1 - r3)):
            v = v.astype(BF)
            zero = jnp.zeros_like(v)
            dst[p, i, 1] = v
            dst[p, i, 0] = jnp.where(lane == 0, zero, pltpu.roll(v, 1, 1))
            dst[p, i, 2] = jnp.where(lane == COLS - 1, zero, pltpu.roll(v, COLS - 1, 1))

    def first_layer(j):
        x = cols_in[:, j * 256:(j + 1) * 256].astype(BF)
        z = jnp.dot(wi, x, preferred_element_type=F32).astype(BF)
        for h in range(2):
            zh = z[:, h * COLS:(h + 1) * COLS]
            row = 2 * j + h
            keep[row] = zh
            row_a[row] = masked(silu(0.5 * zh.astype(F32)), row - 3)
        if j:
            transformed(row_a, act_a, j - 1)

    def product(src, u, pairs, i):
        chunks = []
        for lo, hi in ((0, whole), (whole, chan)):
            for dc in range(3):
                chunks.append(jnp.concatenate([src[p, i, dc, lo:hi] for p in pairs], axis=1))
        return jnp.dot(u[i], jnp.concatenate(chunks, axis=0), preferred_element_type=F32)

    def conv(src, u, pairs, beside, slot):
        for i in range(4):
            prods[slot, i, :, :COLS * len(pairs)] = product(src, u, pairs, i)
            for work in beside[i * len(beside) // 4:(i + 1) * len(beside) // 4]:
                work()

    def untransformed(slot, row):
        at = slice(row // 2 * COLS, (row // 2 + 1) * COLS)
        if row % 2 == 0:
            return prods[slot, 0, :, at] + prods[slot, 1, :, at] + prods[slot, 2, :, at]
        return prods[slot, 1, :, at] - prods[slot, 2, :, at] - prods[slot, 3, :, at]

    def finish_one(row, slot, n):
        y = untransformed(slot, n)
        row_b[row] = masked(silu(y * scale_ref[...] + shift_ref[...]), row - 2)
        if row >= 3 and row % 2:
            transformed(row_b, act_b, (row - 3) // 2)

    acts = {}

    def finish_two(row, slot, n):
        y = untransformed(slot, n)
        second = (keep[row + 2].astype(F32) + y).astype(BF).astype(F32)
        acts[row] = masked(silu(0.5 * second), row - 1).astype(BF)
        if row % 2:
            both = jnp.concatenate([acts.pop(row - 1), acts.pop(row)], axis=1)
            taps_out[row // 2] = jnp.dot(wo_ref[...], both, preferred_element_type=F32)

    pairs_one, pairs_two = (rows + 4) // 2, (rows + 2) // 2
    steps_one = [tuple(range(p, min(p + 2, pairs_one))) for p in range(0, pairs_one, 2)]
    steps_two = [tuple(range(p, min(p + 2, pairs_two))) for p in range(0, pairs_two, 2)]
    ready, slot = 0, 0
    waiting = []
    for pairs in steps_one:
        while ready <= pairs[-1] + 1:
            first_layer(ready)
            ready += 1
        beside = list(waiting)
        for j in range(ready, min(pairs[-1] + 5, pairs_one + 1)):
            beside.append(functools.partial(first_layer, j))
            ready = j + 1
        conv(act_a, u1, pairs, beside, slot)
        waiting = [functools.partial(finish_one, 2 * pairs[0] + n, slot, n) for n in range(2 * len(pairs))]
        slot = 1 - slot
    done = 2 * steps_one[-1][0]
    for pairs in steps_two:
        if 2 * pairs[-1] + 3 >= done:
            for work in waiting:
                work()
            waiting, done = [], 2 * pairs_one
        conv(act_b, u2, pairs, waiting, slot)
        done = 2 * pairs_one
        waiting = [functools.partial(finish_two, 2 * pairs[0] + n, slot, n) for n in range(2 * len(pairs))]
        slot = 1 - slot
    for work in waiting:
        work()

    highs = []
    lane8 = lax.broadcasted_iota(jnp.int32, (TAP_ROWS, COLS), 1)
    for r in range(rows):
        total = None
        for dc in range(3):
            v = None
            for dr in range(3):
                t = 3 * dr + dc
                q = r + dr
                p = taps_out[q // 2, TAP_ROWS * t:TAP_ROWS * (t + 1), q % 2 * COLS:(q % 2 + 1) * COLS]
                v = p if v is None else v + p
            if dc == 0:
                v = jnp.where(lane8 == 0, 0.0, pltpu.roll(v, 1, 1))
            elif dc == 2:
                v = jnp.where(lane8 == COLS - 1, 0.0, pltpu.roll(v, COLS - 1, 1))
            total = v if total is None else total + v
        drift = total[:lat].astype(BF).astype(F32)
        at = slice(r * COLS, (r + 1) * COLS)
        value = factors[2 * slots + 1, :lat] * drift + factors[2 * slots + 2, :lat] * own_rows[HALO + r]
        high = value.astype(BF)
        highs.append(high)
        if last:
            low = (value - high.astype(F32)).astype(BF)
            for n in range(copies):
                out_ref[n, 0, :, at] = high
                out_ref[n, 1, :, at] = low
    if not last:
        for i in range(HALO):
            at = slice(i * COLS, (i + 1) * COLS)
            for k in range(spaces):
                to_first = jnp.where(k <= space, highs[i], highs[HALO + i])
                to_second = jnp.where(k < space, highs[i], highs[HALO + i])
                for t in range(slots):
                    out_ref[k * slots + t, :, at] = to_second if t % 2 else to_first


def drift_call(first, last, copies, slots, spaces, rows, chan, lat, tensors):
    V = pltpu.VMEM
    out = jax.ShapeDtypeStruct((copies, 2, lat, rows * COLS) if last else (copies, lat, HALO * COLS), BF)
    scratch = [
        V((lat, (rows + 8) * COLS), F32), V((48, (rows + 6) * COLS), F32), V((rows + 6, chan, COLS), BF),
        V((rows + 6, chan, COLS), F32), V((rows + 4, chan, COLS), F32), V(((rows + 4) // 2, 4, 3, chan, COLS), BF),
        V(((rows + 2) // 2, 4, 3, chan, COLS), BF), V(((rows + 2) // 2, 9 * TAP_ROWS, 2 * COLS), F32),
        V((2, 4, chan, 2 * COLS), F32),
    ]
    passes = 2 * chan * (3 * chan) * 2 * COLS * (rows + 4 + rows + 2)
    return pl.pallas_call(
        functools.partial(drift_kernel, first, last, copies, slots, spaces, rows),
        out_shape=out,
        in_specs=[VMEM_SPEC] * len(tensors),
        out_specs=VMEM_SPEC,
        scratch_shapes=scratch,
        compiler_params=pltpu.CompilerParams(vmem_limit_bytes=25 << 20),
        cost_estimate=pl.CostEstimate(flops=passes, transcendentals=36 * chan * COLS, bytes_accessed=6 << 20),
        name="drift",
    )(*tensors)


def finish_kernel(slots, sent_one, sent_two, sent_ref, factors, iterate_ref, end_ref):
    rows, lat = iterate_ref.shape[2], iterate_ref.shape[1]
    space = lax.axis_index("space")
    own_rows = start_rows(space, sent_two, sent_one) + start_rows(space, sent_one, sent_two)
    for r in range(rows):
        at = slice(r * COLS, (r + 1) * COLS)
        lower, every = factors[2 * slots, :lat] * own_rows[r], None
        for q in range(slots):
            value = sent_ref[q, 0, :, at].astype(F32) + sent_ref[q, 1, :, at].astype(F32)
            full = factors[slots + q, :lat] * value
            lower = lower + factors[q, :lat] * value
            every = full if every is None else every + full
        iterate_ref[0, :, r, :] = lower
        end_ref[:, r, :] = every


def neighbour_rows(rows):
    count, index = lax.axis_size("space"), lax.axis_index("space")
    even = index % 2 == 0
    head, tail = rows[:, :HALO], rows[:, rows.shape[1] - HALO:]
    swap = lambda begin: [(i + a, i + 1 - a) for i in range(begin, count - 1, 2) for a in (0, 1)]
    one, two = jnp.where(even, tail, head), jnp.where(even, head, tail)
    return one, two, lax.ppermute(one, "space", swap(0)), lax.ppermute(two, "space", swap(1))


def body(latents, owner_slot, slot_steps, step_table, mod_scale, mod_shift, w_in, w_one, w_two, w_out):
    slots, spaces = lax.axis_size("tm"), lax.axis_size("space")
    lat, rows = latents.shape[1], latents.shape[2]
    assert rows == 2 * HALO
    state = neighbour_rows(latents[0])
    call = functools.partial(drift_call, slots=slots, spaces=spaces, rows=rows, chan=w_one.shape[1], lat=lat)
    everyone = slots * spaces
    weights = prep_call(slots, w_one.shape[1], (owner_slot, slot_steps, step_table), (
        mod_scale.T, mod_shift.T, jnp.transpose(w_in, (0, 2, 1)), w_out, w_one, w_two))
    drift = call(True, False, everyone, tensors=(*state, *weights))
    here = lax.axis_index("space").astype(jnp.uint32)
    for picard_step in range(1, ITERS):
        last = picard_step == ITERS - 1
        drift, here = lax.optimization_barrier((drift, here))
        sent = lax.all_to_all(drift, ("space", "tm"), 0, 0).reshape(spaces, slots, lat, HALO * COLS)
        half = lax.dynamic_index_in_dim(sent, here, 0, keepdims=False)
        sent = (sent, lax.ppermute(half, "tm", [(t, t ^ 1) for t in range(slots)]))
        drift = call(False, last, slots if last else everyone, tensors=(*state, *sent, *weights))
    sent = lax.all_to_all(drift, "tm", 0, 0)
    return pl.pallas_call(
        functools.partial(finish_kernel, slots),
        out_shape=(jax.ShapeDtypeStruct(latents.shape, F32), jax.ShapeDtypeStruct(latents.shape[1:], F32)),
        in_specs=[VMEM_SPEC] * 4,
        out_specs=(VMEM_SPEC, VMEM_SPEC),
        compiler_params=pltpu.CompilerParams(vmem_limit_bytes=4 << 20),
        name="finish",
    )(*state[:2], sent, weights[4])


def solution(mesh):
    in_specs = (P("tm", None, "space", None), P(), P(), P(), P(), P(), P(), P(), P(), P())
    out_specs = (P("tm", None, "space", None), P(None, "space", None))
    return jax.shard_map(body, mesh=mesh, in_specs=in_specs, out_specs=out_specs, check_vma=False)
```
